128 devices in a mesh: animal: 16 (over y_lo, x, core), marker: 8 (over z, y_hi).
Axes of the slice: x: 4, y: 4 (y_hi: 2, y_lo: 2; y = y_hi * 2 + y_lo), z: 4, core: 2. Of those that a mesh axis runs over, the one named last changes fastest.
Arguments:
- genotypes: bfloat16 [49152, 25600], P('animal', 'marker'), may hold values from -4 to 4
- direction: bfloat16 [25600, 256], P('marker'), may hold values from -6 to 6
- ridge: float32 [25600], P('marker'), may hold values from 0.5 to 2
- send_list: int32 [16, 16, 2], P('animal'), may hold values from 0 to 23, as said below
- rel_index: int32 [384, 4], P('animal'), may hold values from 0 to 55, as said below
- rel_count: int32 [384], P('animal'), may hold values from 1 to 4, as said below
- rel_prec: bfloat16 [384, 4, 128, 128], P('animal'), may hold values from -0.375 to 0.375
Outputs:
- gradient: float32 [25600, 256], P(('marker', 'animal'))
The draws below stay inside these ranges and needn't reach their ends.
Inputs may be any that keep to these rules, and one draw needn't show every extreme that they name: `send_list`: every entry names one of the sender's own 24 blocks. `rel_index`: entry j of block g indexes g's device's source table; entry 0 is g's own block, g % 24. `rel_count`: the first block of every device has 4 live slots.
All inputs are finite; a program needn't handle non-finite values.
Results may differ from the reference program's by a relative error of at most 0.0033.
Values may be sent and summed in bfloat16 or wider, within the bound.
A program may use at most 128 MiB of HBM per device.

```python
import math
import jax
import jax.numpy as jnp
from jax import lax

MARKERS = 25600
K = 256
BLK = 128
NREL = 4
SLOTS = 2
ANIMALS = 49152
BLOCKS = 384
BLK_DEV = 24


def draw_send_list(key, part):
    peers = BLOCKS // BLK_DEV
    listed = jax.random.randint(jax.random.fold_in(key, 11), (peers, peers, SLOTS), 0, BLK_DEV, dtype=jnp.int32)
    listed = listed.at[:, 0, 0].set(BLK_DEV - 1)
    return listed.at[:, peers - 1, 0].set(0)


def draw_rel_index(key, part):
    peers = BLOCKS // BLK_DEV
    reach = BLK_DEV + peers * SLOTS
    chosen = jax.random.randint(jax.random.fold_in(key, 12), (BLOCKS, NREL), 0, reach, dtype=jnp.int32)
    own_block = jnp.arange(BLOCKS, dtype=jnp.int32) % BLK_DEV
    chosen = chosen.at[:, 0].set(own_block)
    return chosen.at[0, NREL - 1].set(reach - 1)


def draw_rel_count(key, part):
    peers = BLOCKS // BLK_DEV
    heavy = jax.random.randint(jax.random.fold_in(key, 13), (peers,), 0, 2, dtype=jnp.int32)
    even_law = jax.random.randint(jax.random.fold_in(key, 14), (BLOCKS,), 1, NREL + 1, dtype=jnp.int32)
    first_low = jax.random.randint(jax.random.fold_in(key, 15), (BLOCKS,), 0, NREL, dtype=jnp.int32)
    second_low = jax.random.randint(jax.random.fold_in(key, 16), (BLOCKS,), 0, NREL, dtype=jnp.int32)
    low_law = 1 + jnp.minimum(first_low, second_low)
    heavy_block = jnp.repeat(heavy, BLK_DEV)
    counts = jnp.where(heavy_block == 1, even_law, low_law).astype(jnp.int32)
    counts = counts.at[::BLK_DEV].set(NREL)
    return counts.at[BLK_DEV - 1].set(1)


def strengthened(array, rng, source, target, blocks, factor):
    def block_of(dim):
        return (jnp.arange(array.shape[dim]) // (array.shape[dim] // blocks)).reshape((-1,) + (1,) * (array.ndim - 1 - dim))

    near = jax.random.permutation(rng, blocks)[block_of(target)]
    other_side = (block_of(target) + blocks // 2) % blocks
    return jnp.where((block_of(source) == near) | (block_of(source) == other_side), factor * array, array)


def block_scale(own_key, shape, pieces, least, high):
    def one(dim, blocks):
        heights = jax.random.uniform(jax.random.fold_in(jax.random.fold_in(own_key, 6), dim), (blocks,), jnp.float32, least / len(pieces), high / len(pieces))
        return jnp.repeat(jnp.exp(heights), shape[dim] // blocks).reshape((-1,) + (1,) * (len(shape) - dim - 1))

    gain = one(*pieces[0])
    for cut in pieces[1:]:
        gain = gain * one(*cut)
    return gain


def bell_draw(stream_key, extent, scale, limit, pieces=(), kind=jnp.bfloat16):
    entries = jax.random.normal(stream_key, extent, jnp.float32) * scale
    if len(pieces) > 0:
        entries = block_scale(stream_key, extent, pieces, -0.22, 0.18) * entries
    return jnp.clip(entries, min=-limit, max=limit).astype(kind)


def heavy_noise(stream_key, extent, scale, most, pieces, heavy, kind=jnp.bfloat16):
    drawn = scale * jax.random.normal(stream_key, extent, jnp.float32)
    if pieces:
        drawn = drawn * block_scale(stream_key, extent, pieces, -0.22, 0.18)
    return jnp.clip(strengthened(drawn, jax.random.fold_in(stream_key, 3), *heavy), -most, most).astype(kind)


def setup_inputs(seed: int = 0) -> dict:
    splits = jax.random.split(jax.random.key(seed), 8)
    genotypes = heavy_noise(splits[0], (ANIMALS, MARKERS), 1.0, 4.0, ((0, 16), (1, 8)), (0, 1, 16, 2.0))
    direction = bell_draw(splits[1], (MARKERS, K), 1.0, 6.0, ((0, 8),))
    ridge = jnp.clip(jnp.exp(math.log(2.0) - 1.3862944 * jax.random.uniform(splits[2], (MARKERS,), jnp.float32) ** block_scale(splits[2], (MARKERS,), ((0, 8),), -0.2, 0.2)), 0.5, 2.0)
    send_list = draw_send_list(jax.random.fold_in(splits[7], 71), 0)
    rel_index = draw_rel_index(jax.random.fold_in(splits[7], 71), 0)
    rel_count = draw_rel_count(jax.random.fold_in(splits[7], 71), 0)
    rel_prec = bell_draw(splits[6], (BLOCKS, NREL, BLK, BLK), (2 * BLK) ** -0.5, 0.375, ((0, 16),))
    return dict(genotypes=genotypes, direction=direction, ridge=ridge, send_list=send_list, rel_index=rel_index, rel_count=rel_count, rel_prec=rel_prec)


def reference(genotypes, direction, ridge, send_list, rel_index, rel_count, rel_prec):
    animal_sum = (jnp.dot(genotypes, direction, preferred_element_type=jnp.float32) * (1.0 / math.sqrt(MARKERS))).astype(jnp.bfloat16)
    animal_blocks = animal_sum.reshape(BLOCKS, BLK, K)
    owner_dev = (jnp.arange(BLOCKS, dtype=jnp.int32) // BLK_DEV)[:, None]
    far_index = jnp.maximum(rel_index - BLK_DEV, 0).astype(jnp.int32)
    peer_dev = (far_index // SLOTS).astype(jnp.int32)
    slot_index = (far_index % SLOTS).astype(jnp.int32)
    owner_full = jnp.broadcast_to(owner_dev, rel_index.shape).astype(jnp.int32)
    sent_block = send_list[peer_dev, owner_full, slot_index]
    source_block = jnp.where(rel_index < BLK_DEV, owner_full * BLK_DEV + rel_index, peer_dev * BLK_DEV + sent_block).astype(jnp.int32)
    active = jnp.arange(NREL, dtype=jnp.int32)[None, :] < rel_count[:, None]

    def relative_block(packed):
        precision, chosen, active_row = packed
        gathered = animal_blocks[chosen]
        gathered = jnp.where(active_row[:, None, None], gathered, jnp.zeros_like(gathered))
        return jnp.einsum('jrc,jck->rk', precision.astype(jnp.float32), gathered.astype(jnp.float32)).astype(jnp.bfloat16)
    relative_sum = lax.map(relative_block, (rel_prec, source_block, active)).reshape(ANIMALS, K)
    gradient = jnp.dot(genotypes.T, relative_sum, preferred_element_type=jnp.float32) * (1.0 / math.sqrt(ANIMALS))
    return gradient + ridge[:, None] * direction.astype(jnp.float32)
```

```python
import math

import jax
import jax.numpy as jnp
from jax import lax
from jax.experimental import pallas as pl
from jax.experimental.pallas import tpu as pltpu
from jax.sharding import PartitionSpec as P

MESH = pl.DeviceIdType.MESH
MARKERS = 25600
ANIMALS = 49152
BLK = 128
K = 256
NB = 24
NREL = 4
PEERS = 16
SLOTS = 2
ROWS = NB * BLK
COLS = 3200
OWN = 200
KO = 32
CB = 4
W = CB * BLK
NC = NB // CB
F32 = jnp.float32
BF16 = jnp.bfloat16


def kernel(
    geno, direc, prec, send_list, rel_index, rel_count, out,
    g_v, d_v, prec_v, st, r1p, r1m, r2p, r2m, ry, t_loc, table, stage, rt, ot, o_full, cx,
    d1, d2p, d2m, dy, e1p, e1m, e2p, e2m, ey,
    ld_sem, ldg_sem, a_send, a_recv, b_send, b_recv, c_send, c_recv, x_send, x_recv, d_send, d_recv,
):
    a = lax.axis_index("animal")
    m = lax.axis_index("marker")
    z, yh = m // 2, m % 2
    zp, zm, zo = (z + 1) % 4, (z + 3) % 4, (z + 2) % 4
    up, down, across = zp * 2 + yh, zm * 2 + yh, z * 2 + 1 - yh
    yl, x, core = a // 8, (a // 2) % 4, a % 2
    xp, xm, xo = (x + 1) % 4, (x + 3) % 4, (x + 2) % 4
    right, left = yl * 8 + xp * 2 + core, yl * 8 + xm * 2 + core
    beside, sibling = (1 - yl) * 8 + x * 2 + core, yl * 8 + x * 2 + 1 - core

    def load_g(c):
        rows = pl.ds(pl.multiple_of(c * W, W), W)
        return pltpu.make_async_copy(geno.at[rows], g_v.at[rows], ldg_sem.at[c])

    load_d = pltpu.make_async_copy(direc, d_v, ld_sem.at[0])
    load_p = pltpu.make_async_copy(prec, prec_v, ld_sem.at[1])

    def remote(src, dst, send, recv, **device):
        return pltpu.make_async_remote_copy(
            src_ref=src, dst_ref=dst, send_sem=send, recv_sem=recv, device_id=device, device_id_type=MESH
        )

    load_d.start()
    load_g(0).start()
    load_g(1).start()
    barrier = pltpu.get_barrier_semaphore()

    def greet(i, carry):
        pl.semaphore_signal(barrier, inc=1, device_id={"animal": (a + i) % PEERS}, device_id_type=MESH)
        return carry

    lax.fori_loop(1, PEERS, greet, 0)
    for other in (up, down, across):
        pl.semaphore_signal(barrier, inc=1, device_id={"marker": other}, device_id_type=MESH)
    load_d.wait()

    def krows(start, size):
        return pl.ds(pl.multiple_of(start, KO), size)

    def a1p(c):
        return remote(st.at[c, krows(zo * 64, KO)], r1p.at[c], a_send.at[0, c], a_recv.at[0, c], marker=up)

    def a1m(c):
        return remote(st.at[c, krows(zo * 64 + KO, KO)], r1m.at[c], a_send.at[1, c], a_recv.at[1, c], marker=down)

    def a2p(c):
        return remote(st.at[c, krows(zp * 64, 64)], r2p.at[c], a_send.at[2, c], a_recv.at[2, c], marker=up)

    def a2m(c):
        return remote(st.at[c, krows(zm * 64, 64)], r2m.at[c], a_send.at[3, c], a_recv.at[3, c], marker=down)

    def ay(c):
        return remote(
            st.at[c, krows(z * 64 + (1 - yh) * KO, KO)], ry.at[c], a_send.at[4, c], a_recv.at[4, c], marker=across
        )

    def step_a(it, carry):
        @pl.when(it < NC)
        def _():
            c = it

            @pl.when(c + 2 < NC)
            def _():
                load_g(c + 2).start()

            @pl.when(c == NC - 1)
            def _():
                load_p.start()

            load_g(c).wait()
            for half in range(2):
                rows = pl.ds(pl.multiple_of(c * W + half * 256, 256), 256)
                part = jnp.dot(g_v[rows, :], d_v[...], preferred_element_type=F32)
                st[c, :, half * 256 : half * 256 + 256] = part.T

            @pl.when(c == 0)
            def _():
                pl.semaphore_wait(barrier, PEERS - 1 + 3)

            a1p(c).start()
            a1m(c).start()

        @pl.when((it >= 1) & (it < NC + 1))
        def _():
            c = it - 1
            a1p(c).wait_recv()
            own = krows(zp * 64, KO)
            st[c, own] = st[c, own] + r1p[c]
            a2p(c).start()
            a1m(c).wait_recv()
            low = krows(zm * 64 + KO, KO)
            st[c, low] = st[c, low] + r1m[c]
            a2m(c).start()

        @pl.when((it >= 2) & (it < NC + 2))
        def _():
            c = it - 2
            a2p(c).wait_recv()
            a2m(c).wait_recv()
            own = krows(z * 64, 64)
            st[c, own] = st[c, own] + (r2p[c] + r2m[c])
            ay(c).start()

        @pl.when(it >= 3)
        def _():
            c = it - 3
            ay(c).wait_recv()
            done = st[c, krows(z * 64 + yh * KO, KO)] + ry[c]
            done = (done * (1.0 / math.sqrt(MARKERS))).astype(BF16)
            for b in range(CB):
                t_loc[c * CB + b] = done[:, b * BLK : (b + 1) * BLK]
                table[c * CB + b] = done[:, b * BLK : (b + 1) * BLK]

        return carry

    lax.fori_loop(0, NC + 3, step_a, 0)

    def b_copy(e, p):
        return remote(
            stage.at[e], table.at[pl.ds(NB + SLOTS * p, SLOTS)], b_send.at[e], b_recv.at[p], animal=e
        )

    def step_b(i, carry):
        e = (a + i) % PEERS
        for s in range(SLOTS):
            stage[e, s] = t_loc[send_list[0, e, s]]
        b_copy(e, a).start()
        return carry

    lax.fori_loop(1, PEERS, step_b, 0)
    for s in range(SLOTS):
        table[NB + SLOTS * a + s] = t_loc[send_list[0, a, s]]
    load_p.wait()

    def wait_b(i, carry):
        p = (a + i) % PEERS
        b_copy(p, p).wait_recv()
        return carry

    lax.fori_loop(1, PEERS, wait_b, 0)

    def c_copy(kind, c, owner, to):
        rows = krows(owner * KO, KO)
        return remote(rt.at[c, rows], rt.at[c, rows], c_send.at[kind, c], c_recv.at[kind, c], marker=to)

    def gather_in(kind, c):
        owner = (across, zm * 2 + yh, zp * 2 + yh, zm * 2 + 1 - yh, zp * 2 + 1 - yh, zo * 2 + yh, zo * 2 + 1 - yh)[kind]
        return c_copy(kind, c, owner, up)

    ot[...] = jnp.zeros_like(ot)

    def step_c(it, carry):
        @pl.when(it < NC)
        def _():
            c = it
            for b in range(CB):
                g = c * CB + b
                count = rel_count[g]
                picked = []
                for j in range(NREL):
                    block = table[rel_index[g, j]]
                    picked.append(jnp.where(j < count, block, jnp.zeros_like(block)))
                total = lax.dot_general(
                    jnp.concatenate(picked, axis=1),
                    jnp.concatenate([prec_v[g, j] for j in range(NREL)], axis=1),
                    (((1,), (1,)), ((), ())),
                    preferred_element_type=F32,
                )
                rt[c, krows(m * KO, KO), b * BLK : (b + 1) * BLK] = total.astype(BF16)
            c_copy(1, c, m, up).start()
            c_copy(2, c, m, down).start()
            c_copy(0, c, m, across).start()

        @pl.when((it >= 1) & (it < NC + 1))
        def _():
            c = it - 1
            gather_in(0, c).wait_recv()
            c_copy(3, c, across, up).start()
            c_copy(4, c, across, down).start()

        @pl.when((it >= 2) & (it < NC + 2))
        def _():
            c = it - 2
            gather_in(1, c).wait_recv()
            c_copy(5, c, zm * 2 + yh, up).start()
            gather_in(4, c).wait_recv()
            c_copy(6, c, zp * 2 + 1 - yh, down).start()

        @pl.when(it >= 3)
        def _():
            c = it - 3
            for kind in (2, 3, 5, 6):
                gather_in(kind, c).wait_recv()
            rows = pl.ds(pl.multiple_of(c * W, W), W)
            lhs = rt[c]

            def tile(n, inner):
                cols = pl.ds(pl.multiple_of(n * 256, 256), 256)
                ot[:, cols] += jnp.dot(lhs, g_v[rows, cols], preferred_element_type=F32)
                return inner

            lax.fori_loop(0, COLS // 256, tile, 0)
            ot[:, COLS - 128 :] += jnp.dot(lhs, g_v[rows, COLS - 128 :], preferred_element_type=F32)

        return carry

    lax.fori_loop(0, NC + 3, step_c, 0)

    def turn(n, carry):
        cols = pl.ds(pl.multiple_of(n * 128, 128), 128)
        o_full[cols, :] = ot[:, cols].T
        return carry

    lax.fori_loop(0, COLS // 128, turn, 0)

    def owner_rows(q, side):
        return pl.ds(pl.multiple_of((2 * q + side) * OWN, 8), OWN)

    def x_copy(q):
        return remote(o_full.at[owner_rows(q, 1 - core)], cx.at[q], x_send.at[q], x_recv.at[q], animal=sibling)

    order = (xo, 4 + xo, 4 + xp, xm, xp, 4 + xm, x, 4 + x)
    for q in order:
        x_copy(q).start()

    def chip_sum(q):
        x_copy(q).wait_recv()
        return o_full[owner_rows(q, core), :] + cx[q]

    def d_copy(kind):
        src, dst, to = (
            (d1.at[0], e1p, right), (d1.at[1], e1m, left),
            (d2p.at[0], e2p.at[0], right), (d2p.at[1], e2p.at[1], right),
            (d2m.at[0], e2m.at[0], left), (d2m.at[1], e2m.at[1], left),
            (dy, ey, beside),
        )[kind]
        return remote(src, dst, d_send.at[kind], d_recv.at[kind], animal=to)

    d1[0] = chip_sum(xo).astype(BF16)
    d_copy(0).start()
    d1[1] = chip_sum(4 + xo).astype(BF16)
    d_copy(1).start()
    d2p[1] = chip_sum(4 + xp).astype(BF16)
    d_copy(3).start()
    d2m[0] = chip_sum(xm).astype(BF16)
    d_copy(4).start()
    near = chip_sum(xp)
    d_copy(0).wait_recv()
    d2p[0] = (near + e1p[...].astype(F32)).astype(BF16)
    d_copy(2).start()
    near = chip_sum(4 + xm)
    d_copy(1).wait_recv()
    d2m[1] = (near + e1m[...].astype(F32)).astype(BF16)
    d_copy(5).start()
    x_copy(x).wait_recv()
    x_copy(4 + x).wait_recv()
    for kind in (2, 3, 4, 5):
        d_copy(kind).wait_recv()

    def ring_sum(side):
        q = side * 4 + x
        own = o_full[owner_rows(q, core), :] + cx[q]
        return own + e2p[side].astype(F32) + e2m[side].astype(F32)

    dy[...] = ring_sum(1 - yl).astype(BF16)
    d_copy(6).start()
    mine = ring_sum(yl)
    d_copy(6).wait_recv()
    out[...] = mine + ey[...].astype(F32)

    def drain(c, carry):
        for copy in (a1p, a1m, a2p, a2m, ay):
            copy(c).wait_send()
        for kind in range(7):
            c_copy(kind, c, m, up).wait_send()
        return carry

    lax.fori_loop(0, NC, drain, 0)

    def drain_b(i, carry):
        b_copy((a + i) % PEERS, a).wait_send()
        return carry

    lax.fori_loop(1, PEERS, drain_b, 0)
    for q in range(8):
        x_copy(q).wait_send()
    for kind in range(7):
        d_copy(kind).wait_send()


def local(genotypes, direction, ridge, send_list, rel_index, rel_count, rel_prec):
    hbm = pl.BlockSpec(memory_space=pl.ANY)
    smem = pl.BlockSpec(memory_space=pltpu.SMEM)
    vmem = pl.BlockSpec(memory_space=pltpu.VMEM)
    dma = pltpu.SemaphoreType.DMA
    gradient = pl.pallas_call(
        kernel,
        out_shape=jax.ShapeDtypeStruct((OWN, K), F32),
        in_specs=[hbm, hbm, hbm, smem, smem, smem],
        out_specs=vmem,
        scratch_shapes=[
            pltpu.VMEM((ROWS, COLS), BF16),
            pltpu.VMEM((COLS, K), BF16),
            pltpu.VMEM((NB, NREL, BLK, BLK), BF16),
            pltpu.VMEM((NC, K, W), F32),
            pltpu.VMEM((NC, KO, W), F32),
            pltpu.VMEM((NC, KO, W), F32),
            pltpu.VMEM((NC, 64, W), F32),
            pltpu.VMEM((NC, 64, W), F32),
            pltpu.VMEM((NC, KO, W), F32),
            pltpu.VMEM((NB, KO, BLK), BF16),
            pltpu.VMEM((NB + PEERS * SLOTS, KO, BLK), BF16),
            pltpu.VMEM((PEERS, SLOTS, KO, BLK), BF16),
            pltpu.VMEM((NC, K, W), BF16),
            pltpu.VMEM((K, COLS), F32),
            pltpu.VMEM((COLS, K), F32),
            pltpu.VMEM((8, OWN, K), F32),
            pltpu.VMEM((2, OWN, K), BF16),
            pltpu.VMEM((2, OWN, K), BF16),
            pltpu.VMEM((2, OWN, K), BF16),
            pltpu.VMEM((OWN, K), BF16),
            pltpu.VMEM((OWN, K), BF16),
            pltpu.VMEM((OWN, K), BF16),
            pltpu.VMEM((2, OWN, K), BF16),
            pltpu.VMEM((2, OWN, K), BF16),
            pltpu.VMEM((OWN, K), BF16),
            dma((2,)), dma((NC,)),
            dma((5, NC)), dma((5, NC)),
            dma((PEERS,)), dma((PEERS,)),
            dma((7, NC)), dma((7, NC)),
            dma((8,)), dma((8,)),
            dma((7,)), dma((7,)),
        ],
        compiler_params=pltpu.CompilerParams(
            collective_id=0, has_side_effects=True, vmem_limit_bytes=63000000
        ),
    )(genotypes, direction, rel_prec, send_list, rel_index, rel_count)
    row_start = lax.axis_index("animal") * OWN
    own_ridge = lax.dynamic_slice_in_dim(ridge, row_start, OWN, 0)
    own_direction = lax.dynamic_slice_in_dim(direction, row_start, OWN, 0)
    return gradient * (1.0 / math.sqrt(ANIMALS)) + own_ridge[:, None] * own_direction.astype(F32)


def solution(mesh):
    in_specs = (
        P("animal", "marker"),
        P("marker", None),
        P("marker"),
        P("animal", None, None),
        P("animal", None),
        P("animal"),
        P("animal", None, None, None),
    )
    out_specs = P(("marker", "animal"), None)
    return jax.shard_map(local, mesh=mesh, in_specs=in_specs, out_specs=out_specs, check_vma=False)
```

```python
import math

import jax
import jax.numpy as jnp
from jax import lax
from jax.experimental import pallas as pl
from jax.experimental.pallas import tpu as pltpu
from jax.sharding import PartitionSpec as P

MESH = pl.DeviceIdType.MESH
MARKERS = 25600
ANIMALS = 49152
BLK = 128
K = 256
HALF = 128
NB = 24
NREL = 4
PEERS = 16
SLOTS = 2
ROWS = NB * BLK
COLS = 3200
OWN = 200
KO = 16
CB = 4
W = CB * BLK
NC = NB // CB
NI = 2 * NC
F32 = jnp.float32
BF16 = jnp.bfloat16


def kernel(
    geno, direc, prec, send_hbm, index_hbm, rel_count, out,
    g_v, d_v, prec_v, send_list, rel_index, st, r1p, r1m, r2p, r2m, ry, t_loc, table0, table1, stage, rt, ot, o_full, cx,
    d1, d2p, d2m, dy, e1p, e1m, e2p, e2m, ey,
    ld_sem, ldg_sem, a_send, a_recv, b_send, b_recv, c_send, c_recv, x_send, x_recv, d_send, d_recv,
):
    a = lax.axis_index("animal")
    m = lax.axis_index("marker")
    z, yh = m // 2, m % 2
    zp, zm, zo = (z + 1) % 4, (z + 3) % 4, (z + 2) % 4
    up, down, across = zp * 2 + yh, zm * 2 + yh, z * 2 + 1 - yh
    yl, x, core = a // 8, (a // 2) % 4, a % 2
    xp, xm, xo = (x + 1) % 4, (x + 3) % 4, (x + 2) % 4
    right, left = yl * 8 + xp * 2 + core, yl * 8 + xm * 2 + core
    beside, sibling = (1 - yl) * 8 + x * 2 + core, yl * 8 + x * 2 + 1 - core

    tables = (table0, table1)

    def load_g(c):
        rows = pl.ds(pl.multiple_of(c * W, W), W)
        return pltpu.make_async_copy(geno.at[rows], g_v.at[rows], ldg_sem.at[c])

    load_d = pltpu.make_async_copy(direc, d_v, ld_sem.at[0])
    load_p = pltpu.make_async_copy(prec, prec_v, ld_sem.at[1])
    load_s = pltpu.make_async_copy(send_hbm, send_list, ld_sem.at[2])
    load_i = pltpu.make_async_copy(index_hbm, rel_index, ld_sem.at[3])

    def remote(src, dst, send, recv, **device):
        return pltpu.make_async_remote_copy(
            src_ref=src, dst_ref=dst, send_sem=send, recv_sem=recv, device_id=device, device_id_type=MESH
        )

    load_d.start()
    load_g(0).start()
    load_g(1).start()
    barrier = pltpu.get_barrier_semaphore()

    def greet(i, carry):
        pl.semaphore_signal(barrier, inc=1, device_id={"animal": (a + i) % PEERS}, device_id_type=MESH)
        return carry

    lax.fori_loop(1, PEERS, greet, 0)
    for other in (up, down, across):
        pl.semaphore_signal(barrier, inc=1, device_id={"marker": other}, device_id_type=MESH)
    load_s.start()
    load_i.start()
    load_d.wait()

    def krows(i, start, size):
        return pl.ds(pl.multiple_of((i // NC) * HALF + start, KO), size)

    def a1p(i):
        return remote(st.at[i % NC, krows(i, zo * 32, KO)], r1p.at[i], a_send.at[0, i], a_recv.at[0, i], marker=up)

    def a1m(i):
        return remote(st.at[i % NC, krows(i, zo * 32 + KO, KO)], r1m.at[i], a_send.at[1, i], a_recv.at[1, i], marker=down)

    def a2p(i):
        return remote(st.at[i % NC, krows(i, zp * 32, 32)], r2p.at[i], a_send.at[2, i], a_recv.at[2, i], marker=up)

    def a2m(i):
        return remote(st.at[i % NC, krows(i, zm * 32, 32)], r2m.at[i], a_send.at[3, i], a_recv.at[3, i], marker=down)

    def ay(i):
        rows = krows(i, z * 32 + (1 - yh) * KO, KO)
        return remote(st.at[i % NC, rows], ry.at[i], a_send.at[4, i], a_recv.at[4, i], marker=across)

    def product(c):
        load_g(c).wait()
        rows = pl.ds(pl.multiple_of(c * W, W), W)
        st[c] = jnp.dot(g_v[rows, :], d_v[...], preferred_element_type=F32).T

    def reduce1(i):
        a1p(i).start()
        a1m(i).start()

    def reduce2(i):
        a1p(i).wait_recv()
        near = krows(i, zp * 32, KO)
        st[i % NC, near] = st[i % NC, near] + r1p[i]
        a2p(i).start()
        a1m(i).wait_recv()
        near = krows(i, zm * 32 + KO, KO)
        st[i % NC, near] = st[i % NC, near] + r1m[i]
        a2m(i).start()

    def reduce3(i):
        a2p(i).wait_recv()
        a2m(i).wait_recv()
        own = krows(i, z * 32, 32)
        st[i % NC, own] = st[i % NC, own] + (r2p[i] + r2m[i])
        ay(i).start()

    def reduce4(i, h):
        ay(i).wait_recv()
        done = st[i % NC, krows(i, z * 32 + yh * KO, KO)] + ry[i]
        done = (done * (1.0 / math.sqrt(MARKERS))).astype(BF16)
        for b in range(CB):
            t_loc[h, (i % NC) * CB + b] = done[:, b * BLK : (b + 1) * BLK]
            tables[h][(i % NC) * CB + b] = done[:, b * BLK : (b + 1) * BLK]

    def drain_a(i, carry):
        for copy in (a1p, a1m, a2p, a2m, ay):
            copy(i).wait_send()
        return carry

    def b_copy(h, e, p):
        return remote(
            stage.at[h, e], tables[h].at[pl.ds(NB + SLOTS * p, SLOTS)], b_send.at[h, e], b_recv.at[h, p], animal=e
        )

    def relatives_out(h):
        def one(i, carry):
            e = (a + i) % PEERS
            for s in range(SLOTS):
                stage[h, e, s] = t_loc[h, send_list[0, e, s]]
            b_copy(h, e, a).start()
            return carry

        lax.fori_loop(1, PEERS, one, 0)
        for s in range(SLOTS):
            tables[h][NB + SLOTS * a + s] = t_loc[h, send_list[0, a, s]]

    def relatives_in(h):
        def one(i, carry):
            p = (a + i) % PEERS
            b_copy(h, p, p).wait_recv()
            return carry

        lax.fori_loop(1, PEERS, one, 0)

    def drain_b(h):
        def one(i, carry):
            b_copy(h, (a + i) % PEERS, a).wait_send()
            return carry

        lax.fori_loop(1, PEERS, one, 0)

    def c_copy(kind, i, owner, to):
        rows = krows(i, owner * KO, KO)
        return remote(
            rt.at[i % NC, rows], rt.at[i % NC, rows], c_send.at[kind, i], c_recv.at[kind, i], marker=to
        )

    def arrived(kind, i):
        owner = (across, down, up, zm * 2 + 1 - yh, zp * 2 + 1 - yh, zo * 2 + yh, zo * 2 + 1 - yh)[kind]
        c_copy(kind, i, owner, up).wait_recv()

    def relative_sums(h):
        def one(c, carry):
            i = h * NC + c
            for b in range(CB):
                g = c * CB + b
                count = rel_count[g]
                picked = []
                for j in range(NREL):
                    block = tables[h][rel_index[g, j]]
                    picked.append(jnp.where(j < count, block, jnp.zeros_like(block)))
                total = lax.dot_general(
                    jnp.concatenate(picked, axis=1),
                    jnp.concatenate([prec_v[g, j] for j in range(NREL)], axis=1),
                    (((1,), (1,)), ((), ())),
                    preferred_element_type=F32,
                )
                rt[c, krows(i, m * KO, KO), b * BLK : (b + 1) * BLK] = total.astype(BF16)
            c_copy(1, i, m, up).start()
            c_copy(2, i, m, down).start()
            c_copy(0, i, m, across).start()
            return carry

        lax.fori_loop(0, NC, one, 0)

    def gather_y(i):
        arrived(0, i)
        c_copy(3, i, across, up).start()
        c_copy(4, i, across, down).start()

    def gather_relay(i):
        arrived(1, i)
        c_copy(5, i, down, up).start()
        arrived(4, i)
        c_copy(6, i, zp * 2 + 1 - yh, down).start()

    def drain_c(i, carry):
        for kind in range(7):
            c_copy(kind, i, m, up).wait_send()
        return carry

    def marker_part(h, c):
        i = h * NC + c
        for kind in (2, 3, 5, 6):
            arrived(kind, i)
        rows = pl.ds(pl.multiple_of(c * W, W), W)
        return jnp.dot(rt[c, h * HALF : (h + 1) * HALF], g_v[rows, :], preferred_element_type=F32)

    def marker_first(h):
        ot[...] = marker_part(h, 0)

    def marker_next(h, c):
        ot[...] = ot[...] + marker_part(h, c)

    def marker_last(h):
        o_full[h] = (ot[...] + marker_part(h, NC - 1)).T

    def owner_rows(q, side):
        return pl.ds(pl.multiple_of((2 * q + side) * OWN, 8), OWN)

    def x_copy(h, q):
        return remote(
            o_full.at[h, owner_rows(q, 1 - core)], cx.at[h, q], x_send.at[h, q], x_recv.at[h, q], animal=sibling
        )

    def cores_out(h):
        for q in (xo, 4 + xo, 4 + xp, xm, xp, 4 + xm, x, 4 + x):
            x_copy(h, q).start()

    def chip_sum(h, q):
        x_copy(h, q).wait_recv()
        return o_full[h, owner_rows(q, core)] + cx[h, q]

    def d_copy(h, kind):
        src, dst, to = (
            (d1.at[h, 0], e1p.at[h], right), (d1.at[h, 1], e1m.at[h], left),
            (d2p.at[h, 0], e2p.at[h, 0], right), (d2p.at[h, 1], e2p.at[h, 1], right),
            (d2m.at[h, 0], e2m.at[h, 0], left), (d2m.at[h, 1], e2m.at[h, 1], left),
            (dy.at[h], ey.at[h], beside),
        )[kind]
        return remote(src, dst, d_send.at[h, kind], d_recv.at[h, kind], animal=to)

    def ring1(h):
        d1[h, 0] = chip_sum(h, xo).astype(BF16)
        d_copy(h, 0).start()
        d1[h, 1] = chip_sum(h, 4 + xo).astype(BF16)
        d_copy(h, 1).start()
        d2p[h, 1] = chip_sum(h, 4 + xp).astype(BF16)
        d_copy(h, 3).start()
        d2m[h, 0] = chip_sum(h, xm).astype(BF16)
        d_copy(h, 4).start()

    def ring2(h):
        near = chip_sum(h, xp)
        d_copy(h, 0).wait_recv()
        d2p[h, 0] = (near + e1p[h].astype(F32)).astype(BF16)
        d_copy(h, 2).start()
        near = chip_sum(h, 4 + xm)
        d_copy(h, 1).wait_recv()
        d2m[h, 1] = (near + e1m[h].astype(F32)).astype(BF16)
        d_copy(h, 5).start()

    def ring_sum(h, side):
        q = side * 4 + x
        own = o_full[h, owner_rows(q, core)] + cx[h, q]
        return own + e2p[h, side].astype(F32) + e2m[h, side].astype(F32)

    def ring3(h):
        x_copy(h, x).wait_recv()
        x_copy(h, 4 + x).wait_recv()
        for kind in (2, 3, 4, 5):
            d_copy(h, kind).wait_recv()
        dy[h] = ring_sum(h, 1 - yl).astype(BF16)
        d_copy(h, 6).start()

    def finish(h):
        mine = ring_sum(h, yl)
        d_copy(h, 6).wait_recv()
        out[:, h * HALF : (h + 1) * HALF] = mine + ey[h].astype(F32)

    def drain_d(h):
        for q in range(8):
            x_copy(h, q).wait_send()
        for kind in range(7):
            d_copy(h, kind).wait_send()

    def each(count, step):
        def one(i, carry):
            step(i)
            return carry

        lax.fori_loop(0, count, one, 0)

    def step_a(it):
        @pl.when(it < NC)
        def _():
            @pl.when(it + 2 < NC)
            def _():
                load_g(it + 2).start()

            @pl.when(it == NC - 1)
            def _():
                load_p.start()

            product(it)

            @pl.when(it == 0)
            def _():
                pl.semaphore_wait(barrier, PEERS - 1 + 3)

        reduce1(it)
        pl.when(it >= 1)(lambda: reduce2(it - 1))
        pl.when(it >= 2)(lambda: reduce3(it - 2))
        pl.when(it >= 3)(lambda: reduce4(it - 3, 0))

    each(NC + 3, step_a)
    load_s.wait()
    load_i.wait()
    relatives_out(0)

    def step_a2(j):
        it = NC + 3 + j
        reduce1(it)
        reduce2(it - 1)
        reduce3(it - 2)
        reduce4(it - 3, 1)

    each(NI - NC - 3, step_a2)
    load_p.wait()
    relatives_in(0)
    relative_sums(0)
    reduce2(NI - 1)
    reduce3(NI - 2)
    reduce4(NI - 3, 1)
    reduce3(NI - 1)
    reduce4(NI - 2, 1)
    each(NC, gather_y)
    reduce4(NI - 1, 1)
    relatives_out(1)
    each(NC, gather_relay)
    relatives_in(1)
    relative_sums(1)
    marker_first(0)

    def middle(c):
        marker_next(0, c + 1)
        gather_y(NC + c)

    each(NC - 2, middle)
    gather_y(NI - 2)
    gather_y(NI - 1)
    marker_last(0)
    cores_out(0)
    each(NC, lambda c: gather_relay(NC + c))
    ring1(0)
    marker_first(1)
    marker_next(1, 1)
    ring2(0)
    each(2, lambda c: marker_next(1, c + 2))
    ring3(0)
    marker_next(1, NC - 2)
    marker_last(1)
    cores_out(1)
    finish(0)
    ring1(1)
    ring2(1)
    ring3(1)
    finish(1)

    lax.fori_loop(0, NI, drain_a, 0)
    lax.fori_loop(0, NI, drain_c, 0)
    for h in range(2):
        drain_b(h)
        drain_d(h)


def local(genotypes, direction, ridge, send_list, rel_index, rel_count, rel_prec):
    hbm = pl.BlockSpec(memory_space=pl.ANY)
    smem = pl.BlockSpec(memory_space=pltpu.SMEM)
    vmem = pl.BlockSpec(memory_space=pltpu.VMEM)
    dma = pltpu.SemaphoreType.DMA
    gradient = pl.pallas_call(
        kernel,
        out_shape=jax.ShapeDtypeStruct((OWN, K), F32),
        in_specs=[hbm, hbm, hbm, hbm, hbm, smem],
        out_specs=vmem,
        scratch_shapes=[
            pltpu.VMEM((ROWS, COLS), BF16),
            pltpu.VMEM((COLS, K), BF16),
            pltpu.VMEM((NB, NREL, BLK, BLK), BF16),
            pltpu.SMEM((1, PEERS, SLOTS), jnp.int32),
            pltpu.SMEM((NB, NREL), jnp.int32),
            pltpu.VMEM((NC, K, W), F32),
            pltpu.VMEM((NI, KO, W), F32),
            pltpu.VMEM((NI, KO, W), F32),
            pltpu.VMEM((NI, 2 * KO, W), F32),
            pltpu.VMEM((NI, 2 * KO, W), F32),
            pltpu.VMEM((NI, KO, W), F32),
            pltpu.VMEM((2, NB, KO, BLK), BF16),
            pltpu.VMEM((NB + PEERS * SLOTS, KO, BLK), BF16),
            pltpu.VMEM((NB + PEERS * SLOTS, KO, BLK), BF16),
            pltpu.VMEM((2, PEERS, SLOTS, KO, BLK), BF16),
            pltpu.VMEM((NC, K, W), BF16),
            pltpu.VMEM((HALF, COLS), F32),
            pltpu.VMEM((2, COLS, HALF), F32),
            pltpu.VMEM((2, 8, OWN, HALF), F32),
            pltpu.VMEM((2, 2, OWN, HALF), BF16),
            pltpu.VMEM((2, 2, OWN, HALF), BF16),
            pltpu.VMEM((2, 2, OWN, HALF), BF16),
            pltpu.VMEM((2, OWN, HALF), BF16),
            pltpu.VMEM((2, OWN, HALF), BF16),
            pltpu.VMEM((2, OWN, HALF), BF16),
            pltpu.VMEM((2, 2, OWN, HALF), BF16),
            pltpu.VMEM((2, 2, OWN, HALF), BF16),
            pltpu.VMEM((2, OWN, HALF), BF16),
            dma((4,)), dma((NC,)),
            dma((5, NI)), dma((5, NI)),
            dma((2, PEERS)), dma((2, PEERS)),
            dma((7, NI)), dma((7, NI)),
            dma((2, 8)), dma((2, 8)),
            dma((2, 7)), dma((2, 7)),
        ],
        compiler_params=pltpu.CompilerParams(
            collective_id=0, has_side_effects=True, vmem_limit_bytes=63000000
        ),
    )(genotypes, direction, rel_prec, send_list, rel_index, rel_count)
    row_start = lax.axis_index("animal") * OWN
    own_ridge = lax.dynamic_slice_in_dim(ridge, row_start, OWN, 0)
    own_direction = lax.dynamic_slice_in_dim(direction, row_start, OWN, 0)
    return gradient * (1.0 / math.sqrt(ANIMALS)) + own_ridge[:, None] * own_direction.astype(F32)


def solution(mesh):
    in_specs = (
        P("animal", "marker"),
        P("marker", None),
        P("marker"),
        P("animal", None, None),
        P("animal", None),
        P("animal"),
        P("animal", None, None, None),
    )
    out_specs = P(("marker", "animal"), None)
    return jax.shard_map(local, mesh=mesh, in_specs=in_specs, out_specs=out_specs, check_vma=False)
```

```python
import math

import jax
import jax.numpy as jnp
from jax import lax
from jax.experimental import pallas as pl
from jax.experimental.pallas import tpu as pltpu
from jax.sharding import PartitionSpec as P

MESH = pl.DeviceIdType.MESH
MARKERS = 25600
ANIMALS = 49152
BLK = 128
K = 256
HALF = 128
NB = 24
NREL = 4
PEERS = 16
SLOTS = 2
ROWS = NB * BLK
COLS = 3200
OWN = 200
KO = 16
CB = 4
W = CB * BLK
NC = NB // CB
NI = 2 * NC
AWAY = ((1, 2), (0, 2), (1, 1), (1, 3), (0, 1), (0, 3), (1, 0))
F32 = jnp.float32
BF16 = jnp.bfloat16


def kernel(
    geno, direc, own_direc, ridge, prec, send_hbm, index_hbm, rel_count, out,
    g_v, d_v, own_v, ridge_v, ridge_col, prec_v, send_list, rel_index, st, r1p, r1m, r2p, r2m, ry, t_loc, table0, table1, stage, rt, ot, o_full, cx,
    d_out, d_in,
    ld_sem, ldg_sem, a_send, a_recv, b_send, b_recv, c_send, c_recv, x_send, x_recv, d_send, d_recv,
):
    a = lax.axis_index("animal")
    m = lax.axis_index("marker")
    z, yh = m // 2, m % 2
    zp, zm, zo = (z + 1) % 4, (z + 3) % 4, (z + 2) % 4
    up, down, across = zp * 2 + yh, zm * 2 + yh, z * 2 + 1 - yh
    core, mine = a % 2, a // 2
    yl, x = mine // 4, mine % 4
    sibling = 2 * mine + 1 - core
    markers_away = [((z + dz) % 4 * 2 + (yh + dy) % 2, (z + 4 - dz) % 4 * 2 + (yh + dy) % 2) for dy, dz in AWAY]
    animals_away = [(yl + dy) % 2 * 4 + (x + dx) % 4 for dy, dx in AWAY]
    tables = (table0, table1)

    def load_g(c):
        rows = pl.ds(pl.multiple_of(c * W, W), W)
        return pltpu.make_async_copy(geno.at[rows], g_v.at[rows], ldg_sem.at[c])

    load_d = pltpu.make_async_copy(direc, d_v, ld_sem.at[0])
    load_p = pltpu.make_async_copy(prec, prec_v, ld_sem.at[1])
    load_s = pltpu.make_async_copy(send_hbm, send_list, ld_sem.at[2])
    load_i = pltpu.make_async_copy(index_hbm, rel_index, ld_sem.at[3])
    load_o = pltpu.make_async_copy(own_direc.at[a], own_v, ld_sem.at[4])
    load_r = pltpu.make_async_copy(ridge, ridge_v, ld_sem.at[5])

    def remote(src, dst, send, recv, **device):
        return pltpu.make_async_remote_copy(
            src_ref=src, dst_ref=dst, send_sem=send, recv_sem=recv, device_id=device, device_id_type=MESH
        )

    load_d.start()
    load_g(0).start()
    load_g(1).start()
    barrier = pltpu.get_barrier_semaphore()

    def greet(i, carry):
        pl.semaphore_signal(barrier, inc=1, device_id={"animal": (a + i) % PEERS}, device_id_type=MESH)
        return carry

    lax.fori_loop(1, PEERS, greet, 0)
    for other, _ in markers_away:
        pl.semaphore_signal(barrier, inc=1, device_id={"marker": other}, device_id_type=MESH)
    load_s.start()
    load_i.start()
    load_o.start()
    load_r.start()
    load_d.wait()

    def krows(i, start, size):
        return pl.ds(pl.multiple_of((i // NC) * HALF + start, KO), size)

    def a1p(i):
        return remote(st.at[i % NC, krows(i, zo * 32, KO)], r1p.at[i], a_send.at[0, i], a_recv.at[0, i], marker=up)

    def a1m(i):
        return remote(st.at[i % NC, krows(i, zo * 32 + KO, KO)], r1m.at[i], a_send.at[1, i], a_recv.at[1, i], marker=down)

    def a2p(i):
        return remote(st.at[i % NC, krows(i, zp * 32, 32)], r2p.at[i], a_send.at[2, i], a_recv.at[2, i], marker=up)

    def a2m(i):
        return remote(st.at[i % NC, krows(i, zm * 32, 32)], r2m.at[i], a_send.at[3, i], a_recv.at[3, i], marker=down)

    def ay(i):
        rows = krows(i, z * 32 + (1 - yh) * KO, KO)
        return remote(st.at[i % NC, rows], ry.at[i], a_send.at[4, i], a_recv.at[4, i], marker=across)

    def product(c):
        load_g(c).wait()
        rows = pl.ds(pl.multiple_of(c * W, W), W)
        st[c] = jnp.dot(g_v[rows, :], d_v[...], preferred_element_type=F32).T

    def reduce1(i):
        a1p(i).start()
        a1m(i).start()

    def reduce2(i):
        a1p(i).wait_recv()
        near = krows(i, zp * 32, KO)
        st[i % NC, near] = st[i % NC, near] + r1p[i]
        a2p(i).start()
        a1m(i).wait_recv()
        near = krows(i, zm * 32 + KO, KO)
        st[i % NC, near] = st[i % NC, near] + r1m[i]
        a2m(i).start()

    def reduce3(i):
        a2p(i).wait_recv()
        a2m(i).wait_recv()
        own = krows(i, z * 32, 32)
        st[i % NC, own] = st[i % NC, own] + (r2p[i] + r2m[i])
        ay(i).start()

    def reduce4(i, h):
        ay(i).wait_recv()
        done = st[i % NC, krows(i, z * 32 + yh * KO, KO)] + ry[i]
        done = (done * (1.0 / math.sqrt(MARKERS))).astype(BF16)
        for b in range(CB):
            t_loc[h, (i % NC) * CB + b] = done[:, b * BLK : (b + 1) * BLK]
            tables[h][(i % NC) * CB + b] = done[:, b * BLK : (b + 1) * BLK]

    def drain_a(i, carry):
        for copy in (a1p, a1m, a2p, a2m, ay):
            copy(i).wait_send()
        return carry

    def b_copy(h, e, p):
        return remote(
            stage.at[h, e], tables[h].at[pl.ds(NB + SLOTS * p, SLOTS)], b_send.at[h, e], b_recv.at[h, p], animal=e
        )

    def relatives_out(h):
        for i in range(1, PEERS):
            e = (a + i) % PEERS
            for s in range(SLOTS):
                stage[h, e, s] = t_loc[h, send_list[s, e]]
            b_copy(h, e, a).start()
        for s in range(SLOTS):
            tables[h][NB + SLOTS * a + s] = t_loc[h, send_list[s, a]]

    def relatives_in(h):
        def one(i, carry):
            p = (a + i) % PEERS
            b_copy(h, p, p).wait_recv()
            return carry

        lax.fori_loop(1, PEERS, one, 0)

    def drain_b(h):
        def one(i, carry):
            b_copy(h, (a + i) % PEERS, a).wait_send()
            return carry

        lax.fori_loop(1, PEERS, one, 0)

    def c_copy(kind, i, owner):
        rows = krows(i, owner * KO, KO)
        to = markers_away[kind][0]
        return remote(rt.at[i % NC, rows], rt.at[i % NC, rows], c_send.at[kind, i], c_recv.at[kind, i], marker=to)

    def relative_sums(h):
        def one(c, carry):
            i = h * NC + c
            for b in range(CB):
                g = c * CB + b
                count = rel_count[g]
                picked = []
                for j in range(NREL):
                    block = tables[h][rel_index[j, g]]
                    picked.append(jnp.where(j < count, block, jnp.zeros_like(block)))
                total = lax.dot_general(
                    jnp.concatenate(picked, axis=1),
                    jnp.concatenate([prec_v[g, j] for j in range(NREL)], axis=1),
                    (((1,), (1,)), ((), ())),
                    preferred_element_type=F32,
                )
                rt[c, krows(i, m * KO, KO), b * BLK : (b + 1) * BLK] = total.astype(BF16)
            for kind in range(7):
                c_copy(kind, i, m).start()
            return carry

        lax.fori_loop(0, NC, one, 0)

    def drain_c(i, carry):
        for kind in range(7):
            c_copy(kind, i, m).wait_send()
        return carry

    def gather_end(h, c):
        for kind in range(7):
            c_copy(kind, h * NC + c, markers_away[kind][1]).wait_recv()

    def marker_part(h, c):
        rows = pl.ds(pl.multiple_of(c * W, W), W)
        return jnp.dot(rt[c, h * HALF : (h + 1) * HALF], g_v[rows, :], preferred_element_type=F32)

    def marker_first(h):
        ot[...] = marker_part(h, 0)

    def marker_next(h, c):
        ot[...] = ot[...] + marker_part(h, c)

    def marker_last(h):
        o_full[h] = (ot[...] + marker_part(h, NC - 1)).T

    def owner_rows(q, side):
        return pl.ds(pl.multiple_of((2 * q + side) * OWN, 8), OWN)

    def x_copy(h, q):
        return remote(
            o_full.at[h, owner_rows(q, 1 - core)], cx.at[h, q], x_send.at[h, q], x_recv.at[h, q], animal=sibling
        )

    def d_copy(h, q, sender):
        return remote(d_out.at[h, q], d_in.at[h, sender], d_send.at[h, q], d_recv.at[h, sender], animal=2 * q + core)

    def cores_out(h):
        for q in animals_away + [mine]:
            x_copy(h, q).start()

    def chip_sum(h, q):
        x_copy(h, q).wait_recv()
        return o_full[h, owner_rows(q, core)] + cx[h, q]

    def owners_out(h):
        for q in animals_away:
            d_out[h, q] = chip_sum(h, q).astype(BF16)
            d_copy(h, q, mine).start()

    def ridge_column():
        load_r.wait()
        turned = ridge_v[...].T
        for j in range(COLS // BLK):
            ridge_col[j * BLK : (j + 1) * BLK] = turned[:, j : j + 1]

    def finish(h):
        cols = slice(h * HALF, (h + 1) * HALF)
        own = pl.ds(pl.multiple_of(a * OWN, 8), OWN)
        total = chip_sum(h, mine)
        for q in animals_away:
            d_copy(h, q, q).wait_recv()
            total = total + d_in[h, q].astype(F32)
        out[:, cols] = total * (1.0 / math.sqrt(ANIMALS)) + ridge_col[own] * own_v[:, cols].astype(F32)

    def drain_d(h):
        for q in animals_away:
            x_copy(h, q).wait_send()
            d_copy(h, q, mine).wait_send()
        x_copy(h, mine).wait_send()

    def each(count, step):
        def one(i, carry):
            step(i)
            return carry

        lax.fori_loop(0, count, one, 0)

    def step_a(it):
        @pl.when(it < NC)
        def _():
            @pl.when(it + 2 < NC)
            def _():
                load_g(it + 2).start()

            @pl.when(it == NC - 1)
            def _():
                load_p.start()

            product(it)

            @pl.when(it == 0)
            def _():
                pl.semaphore_wait(barrier, PEERS - 1 + len(AWAY))

        reduce1(it)
        pl.when(it >= 2)(lambda: reduce2(it - 2))
        pl.when(it >= 4)(lambda: reduce3(it - 4))
        pl.when(it >= 6)(lambda: reduce4(it - 6, 0))

    each(NI, step_a)
    load_s.wait()
    load_i.wait()
    relatives_out(0)
    for i in (NI - 2, NI - 1):
        reduce2(i)
        reduce3(i - 2)
        reduce4(i - 4, 1)
    ridge_column()
    load_o.wait()
    for i in (NI - 2, NI - 1):
        reduce3(i)
        reduce4(i - 2, 1)
    load_p.wait()
    relatives_in(0)
    relative_sums(0)
    reduce4(NI - 2, 1)
    reduce4(NI - 1, 1)
    relatives_out(1)
    relatives_in(1)
    relative_sums(1)

    def step_m(h, c):
        gather_end(h, c)
        marker_next(h, c)

    gather_end(0, 0)
    marker_first(0)
    each(NC - 2, lambda c: step_m(0, c + 1))
    gather_end(0, NC - 1)
    marker_last(0)
    cores_out(0)
    gather_end(1, 0)
    marker_first(1)
    step_m(1, 1)
    owners_out(0)
    each(NC - 3, lambda c: step_m(1, c + 2))
    gather_end(1, NC - 1)
    marker_last(1)
    cores_out(1)
    finish(0)
    owners_out(1)
    finish(1)

    lax.fori_loop(0, NI, drain_a, 0)
    lax.fori_loop(0, NI, drain_c, 0)
    for h in range(2):
        drain_b(h)
        drain_d(h)


def local(genotypes, direction, ridge, send_list, rel_index, rel_count, rel_prec):
    hbm = pl.BlockSpec(memory_space=pl.ANY)
    smem = pl.BlockSpec(memory_space=pltpu.SMEM)
    vmem = pl.BlockSpec(memory_space=pltpu.VMEM)
    dma = pltpu.SemaphoreType.DMA
    return pl.pallas_call(
        kernel,
        out_shape=jax.ShapeDtypeStruct((OWN, K), F32),
        in_specs=[hbm, hbm, hbm, hbm, hbm, hbm, hbm, smem],
        out_specs=vmem,
        scratch_shapes=[
            pltpu.VMEM((ROWS, COLS), BF16),
            pltpu.VMEM((COLS, K), BF16),
            pltpu.VMEM((OWN, K), BF16),
            pltpu.VMEM((COLS // BLK, BLK), F32),
            pltpu.VMEM((COLS, 1), F32),
            pltpu.VMEM((NB, NREL, BLK, BLK), BF16),
            pltpu.SMEM((SLOTS, PEERS), jnp.int32),
            pltpu.SMEM((NREL, NB), jnp.int32),
            pltpu.VMEM((NC, K, W), F32),
            pltpu.VMEM((NI, KO, W), F32),
            pltpu.VMEM((NI, KO, W), F32),
            pltpu.VMEM((NI, 2 * KO, W), F32),
            pltpu.VMEM((NI, 2 * KO, W), F32),
            pltpu.VMEM((NI, KO, W), F32),
            pltpu.VMEM((2, NB, KO, BLK), BF16),
            pltpu.VMEM((NB + PEERS * SLOTS, KO, BLK), BF16),
            pltpu.VMEM((NB + PEERS * SLOTS, KO, BLK), BF16),
            pltpu.VMEM((2, PEERS, SLOTS, KO, BLK), BF16),
            pltpu.VMEM((NC, K, W), BF16),
            pltpu.VMEM((HALF, COLS), F32),
            pltpu.VMEM((2, COLS, HALF), F32),
            pltpu.VMEM((2, 8, OWN, HALF), F32),
            pltpu.VMEM((2, 8, OWN, HALF), BF16),
            pltpu.VMEM((2, 8, OWN, HALF), BF16),
            dma((6,)), dma((NC,)),
            dma((5, NI)), dma((5, NI)),
            dma((2, PEERS)), dma((2, PEERS)),
            dma((7, NI)), dma((7, NI)),
            dma((2, 8)), dma((2, 8)),
            dma((2, 8)), dma((2, 8)),
        ],
        compiler_params=pltpu.CompilerParams(
            collective_id=0, has_side_effects=True, vmem_limit_bytes=63000000
        ),
    )(
        genotypes,
        direction,
        direction.reshape(PEERS, OWN, K),
        ridge.reshape(COLS // BLK, BLK),
        rel_prec,
        send_list[0].T,
        rel_index.T,
        rel_count,
    )


def solution(mesh):
    in_specs = (
        P("animal", "marker"),
        P("marker", None),
        P("marker"),
        P("animal", None, None),
        P("animal", None),
        P("animal"),
        P("animal", None, None, None),
    )
    out_specs = P(("marker", "animal"), None)
    return jax.shard_map(local, mesh=mesh, in_specs=in_specs, out_specs=out_specs, check_vma=False)
```

```python
import math

import jax
import jax.numpy as jnp
from jax import lax
from jax.experimental import pallas as pl
from jax.experimental.pallas import tpu as pltpu
from jax.sharding import PartitionSpec as P

MESH = pl.DeviceIdType.MESH
MARKERS = 25600
ANIMALS = 49152
BLK = 128
K = 256
HALF = 128
NB = 24
NREL = 4
PEERS = 16
SLOTS = 2
ROWS = NB * BLK
COLS = 3200
OWN = 200
KO = 16
CB = 4
W = CB * BLK
NC = NB // CB
SPLIT = 1664
NI = 2 * NC
YFIRST = (6, 11)
AWAY = ((1, 2), (0, 2), (1, 1), (1, 3), (0, 1), (0, 3), (1, 0))
F32 = jnp.float32
BF16 = jnp.bfloat16


def kernel(
    geno, direc, own_direc, ridge, prec, send_hbm, index_hbm, rel_count, out,
    g_v, d_v, own_v, ridge_v, ridge_col, prec_v, send_list, rel_index, st, r1p, r1m, r2p, r2m, ry, rw, rq, t_loc, table0, table1, stage, rt, ot, o_full, cx,
    d_out, d_in,
    ld_sem, ldg_sem, a_send, a_recv, o_send, o_recv, b_send, b_recv, c_send, c_recv, x_send, x_recv, d_send, d_recv,
):
    a = lax.axis_index("animal")
    m = lax.axis_index("marker")
    z, yh = m // 2, m % 2
    zp, zm, zo = (z + 1) % 4, (z + 3) % 4, (z + 2) % 4
    up, down, across = zp * 2 + yh, zm * 2 + yh, z * 2 + 1 - yh
    core, mine = a % 2, a // 2
    yl, x = mine // 4, mine % 4
    sibling = 2 * mine + 1 - core
    markers_away = [((z + dz) % 4 * 2 + (yh + dy) % 2, (z + 4 - dz) % 4 * 2 + (yh + dy) % 2) for dy, dz in AWAY]
    animals_away = [(yl + dy) % 2 * 4 + (x + dx) % 4 for dy, dx in AWAY]
    tables = (table0, table1)

    def load_g(c):
        rows = pl.ds(pl.multiple_of(c * W, W), W)
        return pltpu.make_async_copy(geno.at[rows], g_v.at[rows], ldg_sem.at[c])

    load_d = pltpu.make_async_copy(direc, d_v, ld_sem.at[0])
    load_p = pltpu.make_async_copy(prec, prec_v, ld_sem.at[1])
    load_s = pltpu.make_async_copy(send_hbm, send_list, ld_sem.at[2])
    load_i = pltpu.make_async_copy(index_hbm, rel_index, ld_sem.at[3])
    load_o = pltpu.make_async_copy(own_direc.at[a], own_v, ld_sem.at[4])
    load_r = pltpu.make_async_copy(ridge, ridge_v, ld_sem.at[5])

    def remote(src, dst, send, recv, **device):
        return pltpu.make_async_remote_copy(
            src_ref=src, dst_ref=dst, send_sem=send, recv_sem=recv, device_id=device, device_id_type=MESH
        )

    load_d.start()
    load_g(0).start()
    barrier = pltpu.get_barrier_semaphore()

    def greet(i, carry):
        pl.semaphore_signal(barrier, inc=1, device_id={"animal": (a + i) % PEERS}, device_id_type=MESH)
        return carry

    lax.fori_loop(1, PEERS, greet, 0)
    for other, _ in markers_away:
        pl.semaphore_signal(barrier, inc=1, device_id={"marker": other}, device_id_type=MESH)
    load_s.start()
    load_i.start()
    load_o.start()
    load_r.start()
    load_d.wait()
    load_g(1).start()

    def krows(i, start, size):
        return pl.ds(pl.multiple_of((i // NC) * HALF + start, KO), size)

    def a1p(i):
        return remote(st.at[i % NC, krows(i, zo * 32, KO)], r1p.at[i], a_send.at[0, i], a_recv.at[0, i], marker=up)

    def a1m(i):
        return remote(st.at[i % NC, krows(i, zo * 32 + KO, KO)], r1m.at[i], a_send.at[1, i], a_recv.at[1, i], marker=down)

    def a2p(i):
        return remote(st.at[i % NC, krows(i, zp * 32, 32)], r2p.at[i], a_send.at[2, i], a_recv.at[2, i], marker=up)

    def a2m(i):
        return remote(st.at[i % NC, krows(i, zm * 32, 32)], r2m.at[i], a_send.at[3, i], a_recv.at[3, i], marker=down)

    def ay(i):
        rows = krows(i, z * 32 + (1 - yh) * KO, KO)
        return remote(st.at[i % NC, rows], ry.at[i], a_send.at[4, i], a_recv.at[4, i], marker=across)

    def product(c):
        load_g(c).wait()
        rows = pl.ds(pl.multiple_of(c * W, W), W)
        st[c] = jnp.dot(g_v[rows, :], d_v[...], preferred_element_type=F32).T

    def reduce1(i):
        a1p(i).start()
        a1m(i).start()

    def reduce2(i):
        a1p(i).wait_recv()
        near = krows(i, zp * 32, KO)
        st[i % NC, near] = st[i % NC, near] + r1p[i]
        a2p(i).start()
        a1m(i).wait_recv()
        near = krows(i, zm * 32 + KO, KO)
        st[i % NC, near] = st[i % NC, near] + r1m[i]
        a2m(i).start()

    def reduce3(i):
        a2p(i).wait_recv()
        a2m(i).wait_recv()
        own = krows(i, z * 32, 32)
        st[i % NC, own] = st[i % NC, own] + (r2p[i] + r2m[i])
        ay(i).start()

    def settle(h, c, done):
        done = (done * (1.0 / math.sqrt(MARKERS))).astype(BF16)
        for b in range(CB):
            t_loc[h, c * CB + b] = done[:, b * BLK : (b + 1) * BLK]
            tables[h][c * CB + b] = done[:, b * BLK : (b + 1) * BLK]

    def reduce4(i, h):
        ay(i).wait_recv()
        settle(h, i % NC, st[i % NC, krows(i, z * 32 + yh * KO, KO)] + ry[i])

    def o_copy(kind, i):
        u = YFIRST.index(i)
        if kind < 4:
            src, dst, to = krows(i, kind * 32 + (1 - yh) * KO, KO), rw.at[u, kind], across
        else:
            to_z = (zo, zp, zm)[kind - 4]
            src, dst, to = krows(i, to_z * 32 + yh * KO, KO), rq.at[u, kind - 4], to_z * 2 + yh
        return remote(st.at[i % NC, src], dst, o_send.at[kind, u], o_recv.at[kind, u], marker=to)

    def yfirst1(i):
        for kind in range(4):
            o_copy(kind, i).start()

    def yfirst2(i):
        u = YFIRST.index(i)
        for kind in range(4):
            o_copy(kind, i).wait_recv()
            own = krows(i, kind * 32 + yh * KO, KO)
            st[i % NC, own] = st[i % NC, own] + rw[u, kind]
        for kind in range(4, 7):
            o_copy(kind, i).start()

    def yfirst3(i, h):
        u = YFIRST.index(i)
        for kind in range(4, 7):
            o_copy(kind, i).wait_recv()
        own = st[i % NC, krows(i, z * 32 + yh * KO, KO)]
        settle(h, i % NC, own + rq[u, 0] + (rq[u, 1] + rq[u, 2]))

    def drain_a():
        for i in range(NI):
            if i in YFIRST:
                for kind in range(7):
                    o_copy(kind, i).wait_send()
            else:
                for copy in (a1p, a1m, a2p, a2m, ay):
                    copy(i).wait_send()

    def b_copy(h, e, p):
        return remote(
            stage.at[h, e], tables[h].at[pl.ds(NB + SLOTS * p, SLOTS)], b_send.at[h, e], b_recv.at[h, p], animal=e
        )

    def relatives_out(h):
        for i in range(1, PEERS):
            e = (a + i) % PEERS
            for s in range(SLOTS):
                stage[h, e, s] = t_loc[h, send_list[s, e]]
            b_copy(h, e, a).start()
        for s in range(SLOTS):
            tables[h][NB + SLOTS * a + s] = t_loc[h, send_list[s, a]]

    def relatives_in(h):
        def one(i, carry):
            p = (a + i) % PEERS
            b_copy(h, p, p).wait_recv()
            return carry

        lax.fori_loop(1, PEERS, one, 0)

    def drain_b(h):
        def one(i, carry):
            b_copy(h, (a + i) % PEERS, a).wait_send()
            return carry

        lax.fori_loop(1, PEERS, one, 0)

    def c_copy(kind, i, owner):
        rows = krows(i, owner * KO, KO)
        to = markers_away[kind][0]
        return remote(rt.at[i % NC, rows], rt.at[i % NC, rows], c_send.at[kind, i], c_recv.at[kind, i], marker=to)

    def relative_sums(h):
        def one(c, carry):
            i = h * NC + c
            for b in range(CB):
                g = c * CB + b
                count = rel_count[g]
                picked = []
                for j in range(NREL):
                    block = tables[h][rel_index[j, g]]
                    picked.append(jnp.where(j < count, block, jnp.zeros_like(block)))
                total = lax.dot_general(
                    jnp.concatenate(picked, axis=1),
                    jnp.concatenate([prec_v[g, j] for j in range(NREL)], axis=1),
                    (((1,), (1,)), ((), ())),
                    preferred_element_type=F32,
                )
                rt[c, krows(i, m * KO, KO), b * BLK : (b + 1) * BLK] = total.astype(BF16)
            for kind in range(7):
                c_copy(kind, i, m).start()
            return carry

        lax.fori_loop(0, NC, one, 0)

    def drain_c(i, carry):
        for kind in range(7):
            c_copy(kind, i, m).wait_send()
        return carry

    def gather_end(h, c):
        for kind in range(7):
            c_copy(kind, h * NC + c, markers_away[kind][1]).wait_recv()

    def marker_part(h, c):
        rows = pl.ds(pl.multiple_of(c * W, W), W)
        return jnp.dot(rt[c, h * HALF : (h + 1) * HALF], g_v[rows, :], preferred_element_type=F32)

    def marker_first(h):
        ot[...] = marker_part(h, 0)

    def marker_next(h, c):
        ot[...] = ot[...] + marker_part(h, c)

    def owner_rows(q, side):
        return pl.ds(pl.multiple_of((2 * q + side) * OWN, 8), OWN)

    def x_copy(h, q):
        return remote(
            o_full.at[h, owner_rows(q, 1 - core)], cx.at[h, q], x_send.at[h, q], x_recv.at[h, q], animal=sibling
        )

    def d_copy(h, q, sender):
        return remote(d_out.at[h, q], d_in.at[h, sender], d_send.at[h, q], d_recv.at[h, sender], animal=2 * q + core)

    def marker_last(h):
        rows = slice((NC - 1) * W, NC * W)
        for lo, hi, side in ((0, SPLIT, 0), (SPLIT, COLS, 1)):
            part = jnp.dot(rt[NC - 1, h * HALF : (h + 1) * HALF], g_v[rows, lo:hi], preferred_element_type=F32)
            o_full[h, lo:hi] = (ot[:, lo:hi] + part).T
            for k in (2, 1, 3, 0):
                x_copy(h, side * 4 + (x + k) % 4).start()

    def chip_sum(h, q):
        x_copy(h, q).wait_recv()
        return o_full[h, owner_rows(q, core)] + cx[h, q]

    def owners_out(h):
        for q in animals_away:
            d_out[h, q] = chip_sum(h, q).astype(BF16)
            d_copy(h, q, mine).start()

    def ridge_column():
        load_r.wait()
        turned = ridge_v[...].T
        for j in range(COLS // BLK):
            ridge_col[j * BLK : (j + 1) * BLK] = turned[:, j : j + 1]

    def finish(h):
        cols = slice(h * HALF, (h + 1) * HALF)
        own = pl.ds(pl.multiple_of(a * OWN, 8), OWN)
        total = chip_sum(h, mine)
        for q in animals_away:
            d_copy(h, q, q).wait_recv()
            total = total + d_in[h, q].astype(F32)
        out[:, cols] = total * (1.0 / math.sqrt(ANIMALS)) + ridge_col[own] * own_v[:, cols].astype(F32)

    def drain_d(h):
        for q in animals_away:
            x_copy(h, q).wait_send()
            d_copy(h, q, mine).wait_send()
        x_copy(h, mine).wait_send()

    def each(count, step):
        def one(i, carry):
            step(i)
            return carry

        lax.fori_loop(0, count, one, 0)

    def step_a(it):
        @pl.when(it + 2 < NC)
        def _():
            load_g(it + 2).start()

        @pl.when(it == NC - 2)
        def _():
            load_p.start()

        product(it)

        @pl.when(it == 0)
        def _():
            pl.semaphore_wait(barrier, PEERS - 1 + len(AWAY))

        reduce1(it)
        pl.when(it >= 2)(lambda: reduce2(it - 2))
        pl.when(it >= 4)(lambda: reduce3(it - 4))

    each(NC, step_a)
    for it in range(NC, NI + 6):
        for i, ring, straight in (
            (it, reduce1, yfirst1),
            (it - 2, reduce2, yfirst2),
            (it - 4, reduce3, lambda i: yfirst3(i, i // NC)),
            (it - 6, lambda i: reduce4(i, i // NC), None),
        ):
            if i < NI and i not in YFIRST:
                ring(i)
            elif i < NI and straight is not None:
                straight(i)
        if it == 2 * NC - 1:
            load_s.wait()
            load_i.wait()
            relatives_out(0)
        if it == 2 * NC:
            ridge_column()
            load_o.wait()
        if it == 2 * NC + 2:
            load_p.wait()
            relatives_in(0)
            relative_sums(0)
    relatives_out(1)
    relatives_in(1)
    relative_sums(1)

    def step_m(h, c):
        gather_end(h, c)
        marker_next(h, c)

    gather_end(0, 0)
    marker_first(0)
    each(NC - 2, lambda c: step_m(0, c + 1))
    gather_end(0, NC - 1)
    marker_last(0)
    gather_end(1, 0)
    marker_first(1)
    owners_out(0)
    each(NC - 2, lambda c: step_m(1, c + 1))
    gather_end(1, NC - 1)
    marker_last(1)
    owners_out(1)
    finish(0)
    finish(1)

    drain_a()
    lax.fori_loop(0, NI, drain_c, 0)
    for h in range(2):
        drain_b(h)
        drain_d(h)


def local(genotypes, direction, ridge, send_list, rel_index, rel_count, rel_prec):
    hbm = pl.BlockSpec(memory_space=pl.ANY)
    smem = pl.BlockSpec(memory_space=pltpu.SMEM)
    vmem = pl.BlockSpec(memory_space=pltpu.VMEM)
    dma = pltpu.SemaphoreType.DMA
    return pl.pallas_call(
        kernel,
        out_shape=jax.ShapeDtypeStruct((OWN, K), F32),
        in_specs=[hbm, hbm, hbm, hbm, hbm, hbm, hbm, smem],
        out_specs=vmem,
        scratch_shapes=[
            pltpu.VMEM((ROWS, COLS), BF16),
            pltpu.VMEM((COLS, K), BF16),
            pltpu.VMEM((OWN, K), BF16),
            pltpu.VMEM((COLS // BLK, BLK), F32),
            pltpu.VMEM((COLS, 1), F32),
            pltpu.VMEM((NB, NREL, BLK, BLK), BF16),
            pltpu.SMEM((SLOTS, PEERS), jnp.int32),
            pltpu.SMEM((NREL, NB), jnp.int32),
            pltpu.VMEM((NC, K, W), F32),
            pltpu.VMEM((NI, KO, W), F32),
            pltpu.VMEM((NI, KO, W), F32),
            pltpu.VMEM((NI, 2 * KO, W), F32),
            pltpu.VMEM((NI, 2 * KO, W), F32),
            pltpu.VMEM((NI, KO, W), F32),
            pltpu.VMEM((len(YFIRST), 4, KO, W), F32),
            pltpu.VMEM((len(YFIRST), 3, KO, W), F32),
            pltpu.VMEM((2, NB, KO, BLK), BF16),
            pltpu.VMEM((NB + PEERS * SLOTS, KO, BLK), BF16),
            pltpu.VMEM((NB + PEERS * SLOTS, KO, BLK), BF16),
            pltpu.VMEM((2, PEERS, SLOTS, KO, BLK), BF16),
            pltpu.VMEM((NC, K, W), BF16),
            pltpu.VMEM((HALF, COLS), F32),
            pltpu.VMEM((2, COLS, HALF), F32),
            pltpu.VMEM((2, 8, OWN, HALF), F32),
            pltpu.VMEM((2, 8, OWN, HALF), BF16),
            pltpu.VMEM((2, 8, OWN, HALF), BF16),
            dma((6,)), dma((NC,)),
            dma((5, NI)), dma((5, NI)),
            dma((7, len(YFIRST))), dma((7, len(YFIRST))),
            dma((2, PEERS)), dma((2, PEERS)),
            dma((7, NI)), dma((7, NI)),
            dma((2, 8)), dma((2, 8)),
            dma((2, 8)), dma((2, 8)),
        ],
        compiler_params=pltpu.CompilerParams(
            collective_id=0, has_side_effects=True, vmem_limit_bytes=63000000
        ),
    )(
        genotypes,
        direction,
        direction.reshape(PEERS, OWN, K),
        ridge.reshape(COLS // BLK, BLK),
        rel_prec,
        send_list[0].T,
        rel_index.T,
        rel_count,
    )


def solution(mesh):
    in_specs = (
        P("animal", "marker"),
        P("marker", None),
        P("marker"),
        P("animal", None, None),
        P("animal", None),
        P("animal"),
        P("animal", None, None, None),
    )
    out_specs = P(("marker", "animal"), None)
    return jax.shard_map(local, mesh=mesh, in_specs=in_specs, out_specs=out_specs, check_vma=False)
```

```python
import math

import jax
import jax.numpy as jnp
from jax import lax
from jax.experimental import pallas as pl
from jax.experimental.pallas import tpu as pltpu
from jax.sharding import PartitionSpec as P

MESH = pl.DeviceIdType.MESH
MARKERS = 25600
ANIMALS = 49152
BLK = 128
K = 256
HALF = 128
NB = 24
NREL = 4
PEERS = 16
SLOTS = 2
ROWS = NB * BLK
COLS = 3200
OWN = 200
KO = 16
CB = 4
W = CB * BLK
NC = NB // CB
SPLIT = 1664
NI = 2 * NC
YFIRST = (6, 11)
AWAY = ((1, 2), (0, 2), (1, 1), (1, 3), (0, 1), (0, 3), (1, 0))
ALONG_Y = 6
RELAYED = ((2, 4), (3, 5), (0, 1))
F32 = jnp.float32
BF16 = jnp.bfloat16


def kernel(
    geno, direc, own_direc, ridge, prec, send_hbm, index_hbm, rel_count, out,
    g_v, d_v, own_v, ridge_v, ridge_col, prec_v, send_list, rel_index, st, r1p, r1m, r2p, r2m, ry, rw, rq, t_loc, table0, table1, stage, rt, ot, o_full, cx,
    d_out, d_in,
    ld_sem, ldg_sem, a_send, a_recv, o_send, o_recv, b_send, b_recv, c_send, c_recv, x_send, x_recv, d_send, d_recv,
):
    a = lax.axis_index("animal")
    m = lax.axis_index("marker")
    z, yh = m // 2, m % 2
    zp, zm, zo = (z + 1) % 4, (z + 3) % 4, (z + 2) % 4
    up, down, across = zp * 2 + yh, zm * 2 + yh, z * 2 + 1 - yh
    core, mine = a % 2, a // 2
    yl, x = mine // 4, mine % 4
    sibling = 2 * mine + 1 - core
    markers_away = [((z + dz) % 4 * 2 + (yh + dy) % 2, (z + 4 - dz) % 4 * 2 + (yh + dy) % 2) for dy, dz in AWAY]
    animals_away = [(yl + dy) % 2 * 4 + (x + dx) % 4 for dy, dx in AWAY]
    tables = (table0, table1)

    def load_g(c):
        rows = pl.ds(pl.multiple_of(c * W, W), W)
        return pltpu.make_async_copy(geno.at[rows], g_v.at[rows], ldg_sem.at[c])

    load_d = pltpu.make_async_copy(direc, d_v, ld_sem.at[0])
    load_p = pltpu.make_async_copy(prec, prec_v, ld_sem.at[1])
    load_s = pltpu.make_async_copy(send_hbm, send_list, ld_sem.at[2])
    load_i = pltpu.make_async_copy(index_hbm, rel_index, ld_sem.at[3])
    load_o = pltpu.make_async_copy(own_direc.at[a], own_v, ld_sem.at[4])
    load_r = pltpu.make_async_copy(ridge, ridge_v, ld_sem.at[5])

    def remote(src, dst, send, recv, **device):
        return pltpu.make_async_remote_copy(
            src_ref=src, dst_ref=dst, send_sem=send, recv_sem=recv, device_id=device, device_id_type=MESH
        )

    load_d.start()
    load_g(0).start()
    barrier = pltpu.get_barrier_semaphore()

    def greet(i, carry):
        pl.semaphore_signal(barrier, inc=1, device_id={"animal": (a + i) % PEERS}, device_id_type=MESH)
        return carry

    lax.fori_loop(1, PEERS, greet, 0)
    for other, _ in markers_away:
        pl.semaphore_signal(barrier, inc=1, device_id={"marker": other}, device_id_type=MESH)
    load_s.start()
    load_i.start()
    load_o.start()
    load_r.start()
    load_d.wait()
    load_g(1).start()

    def krows(i, start, size):
        return pl.ds(pl.multiple_of((i // NC) * HALF + start, KO), size)

    def a1p(i):
        return remote(st.at[i % NC, krows(i, zo * 32, KO)], r1p.at[i], a_send.at[0, i], a_recv.at[0, i], marker=up)

    def a1m(i):
        return remote(st.at[i % NC, krows(i, zo * 32 + KO, KO)], r1m.at[i], a_send.at[1, i], a_recv.at[1, i], marker=down)

    def a2p(i):
        return remote(st.at[i % NC, krows(i, zp * 32, 32)], r2p.at[i], a_send.at[2, i], a_recv.at[2, i], marker=up)

    def a2m(i):
        return remote(st.at[i % NC, krows(i, zm * 32, 32)], r2m.at[i], a_send.at[3, i], a_recv.at[3, i], marker=down)

    def ay(i):
        rows = krows(i, z * 32 + (1 - yh) * KO, KO)
        return remote(st.at[i % NC, rows], ry.at[i], a_send.at[4, i], a_recv.at[4, i], marker=across)

    def product(c):
        load_g(c).wait()
        rows = pl.ds(pl.multiple_of(c * W, W), W)
        st[c] = jnp.dot(g_v[rows, :], d_v[...], preferred_element_type=F32).T

    def reduce1(i):
        a1p(i).start()
        a1m(i).start()

    def reduce2(i):
        a1p(i).wait_recv()
        near = krows(i, zp * 32, KO)
        st[i % NC, near] = st[i % NC, near] + r1p[i]
        a2p(i).start()
        a1m(i).wait_recv()
        near = krows(i, zm * 32 + KO, KO)
        st[i % NC, near] = st[i % NC, near] + r1m[i]
        a2m(i).start()

    def reduce3(i):
        a2p(i).wait_recv()
        a2m(i).wait_recv()
        own = krows(i, z * 32, 32)
        st[i % NC, own] = st[i % NC, own] + (r2p[i] + r2m[i])
        ay(i).start()

    def settle(h, c, done):
        done = (done * (1.0 / math.sqrt(MARKERS))).astype(BF16)
        for b in range(CB):
            t_loc[h, c * CB + b] = done[:, b * BLK : (b + 1) * BLK]
            tables[h][c * CB + b] = done[:, b * BLK : (b + 1) * BLK]

    def reduce4(i, h):
        ay(i).wait_recv()
        settle(h, i % NC, st[i % NC, krows(i, z * 32 + yh * KO, KO)] + ry[i])

    def o_copy(kind, i):
        u = YFIRST.index(i)
        if kind < 4:
            src, dst, to = krows(i, kind * 32 + (1 - yh) * KO, KO), rw.at[u, kind], across
        else:
            to_z = (zo, zp, zm)[kind - 4]
            src, dst, to = krows(i, to_z * 32 + yh * KO, KO), rq.at[u, kind - 4], to_z * 2 + yh
        return remote(st.at[i % NC, src], dst, o_send.at[kind, u], o_recv.at[kind, u], marker=to)

    def yfirst1(i):
        for kind in range(4):
            o_copy(kind, i).start()

    def yfirst2(i):
        u = YFIRST.index(i)
        for kind in range(4):
            o_copy(kind, i).wait_recv()
            own = krows(i, kind * 32 + yh * KO, KO)
            st[i % NC, own] = st[i % NC, own] + rw[u, kind]
        for kind in range(4, 7):
            o_copy(kind, i).start()

    def yfirst3(i, h):
        u = YFIRST.index(i)
        for kind in range(4, 7):
            o_copy(kind, i).wait_recv()
        own = st[i % NC, krows(i, z * 32 + yh * KO, KO)]
        settle(h, i % NC, own + rq[u, 0] + (rq[u, 1] + rq[u, 2]))

    def drain_a():
        for i in range(NI):
            if i in YFIRST:
                for kind in range(7):
                    o_copy(kind, i).wait_send()
            else:
                for copy in (a1p, a1m, a2p, a2m, ay):
                    copy(i).wait_send()

    def b_copy(h, e, p):
        return remote(
            stage.at[h, e], tables[h].at[pl.ds(NB + SLOTS * p, SLOTS)], b_send.at[h, e], b_recv.at[h, p], animal=e
        )

    def relatives_out(h):
        for i in range(1, PEERS):
            e = (a + i) % PEERS
            for s in range(SLOTS):
                stage[h, e, s] = t_loc[h, send_list[s, e]]
            b_copy(h, e, a).start()
        for s in range(SLOTS):
            tables[h][NB + SLOTS * a + s] = t_loc[h, send_list[s, a]]

    def relatives_in(h):
        def one(i, carry):
            p = (a + i) % PEERS
            b_copy(h, p, p).wait_recv()
            return carry

        lax.fori_loop(1, PEERS, one, 0)

    def drain_b(h):
        def one(i, carry):
            b_copy(h, (a + i) % PEERS, a).wait_send()
            return carry

        lax.fori_loop(1, PEERS, one, 0)

    def c_copy(kind, i, owner, to):
        rows = krows(i // NC * NC, owner // 2 * 32 + owner % 2 * KO, KO)
        return remote(rt.at[i % NC, rows], rt.at[i % NC, rows], c_send.at[kind, i], c_recv.at[kind, i], marker=to)

    def c_out(kind, i):
        return c_copy(kind, i, m, markers_away[kind][0])

    def c_in(kind, i):
        return c_copy(kind, i, markers_away[kind][1], m)

    def c_relay(kind, i, zfirst):
        dz = AWAY[kind][1]
        if zfirst:
            return c_copy(kind, i, (z + 4 - dz) % 4 * 2 + yh, across)
        return c_copy(kind, i, across, (z + dz) % 4 * 2 + yh)

    def relay(i, zfirst):
        if not zfirst:
            c_in(ALONG_Y, i).wait_recv()
        for kind, came in RELAYED:
            if zfirst:
                c_in(came, i).wait_recv()
            c_relay(kind, i, zfirst).start()

    def relative_sums(h):
        def one(c, carry):
            i = h * NC + c
            for b in range(CB):
                g = c * CB + b
                count = rel_count[g]
                picked = []
                for j in range(NREL):
                    block = tables[h][rel_index[j, g]]
                    picked.append(jnp.where(j < count, block, jnp.zeros_like(block)))
                total = lax.dot_general(
                    jnp.concatenate(picked, axis=1),
                    jnp.concatenate([prec_v[g, j] for j in range(NREL)], axis=1),
                    (((1,), (1,)), ((), ())),
                    preferred_element_type=F32,
                )
                rt[c, krows(i, m * KO, KO), b * BLK : (b + 1) * BLK] = total.astype(BF16)
            for kind in (1, 4, 5, 6):
                c_out(kind, i).start()

            @pl.when(c == NC - 1)
            def _():
                for kind, _ in RELAYED:
                    c_out(kind, i).start()

            return carry

        lax.fori_loop(0, NC, one, 0)

    def drain_c(i, carry):
        for kind in range(7):
            c_out(kind, i).wait_send()
        return carry

    def gather_end(h, c):
        i = h * NC + c

        @pl.when(c == NC - 1)
        def _():
            for kind in range(7):
                c_in(kind, i).wait_recv()

        @pl.when((c < NC - 1) & (c % 2 == 0))
        def _():
            for kind in (0, 2, 3, ALONG_Y):
                c_in(kind, i).wait_recv()

        @pl.when((c < NC - 1) & (c % 2 == 1))
        def _():
            for kind in (0, 1, 2, 3, 4, 5):
                c_in(kind, i).wait_recv()

    def marker_part(h, c):
        rows = pl.ds(pl.multiple_of(c * W, W), W)
        return jnp.dot(rt[c, h * HALF : (h + 1) * HALF], g_v[rows, :], preferred_element_type=F32)

    def marker_first(h):
        ot[...] = marker_part(h, 0)

    def marker_next(h, c):
        ot[...] = ot[...] + marker_part(h, c)

    def owner_rows(q, side):
        return pl.ds(pl.multiple_of((2 * q + side) * OWN, 8), OWN)

    def x_copy(h, q):
        return remote(
            o_full.at[h, owner_rows(q, 1 - core)], cx.at[h, q], x_send.at[h, q], x_recv.at[h, q], animal=sibling
        )

    def d_copy(h, q, sender):
        return remote(d_out.at[h, q], d_in.at[h, sender], d_send.at[h, q], d_recv.at[h, sender], animal=2 * q + core)

    def marker_last(h):
        rows = slice((NC - 1) * W, NC * W)
        for lo, hi, side in ((0, SPLIT, 0), (SPLIT, COLS, 1)):
            part = jnp.dot(rt[NC - 1, h * HALF : (h + 1) * HALF], g_v[rows, lo:hi], preferred_element_type=F32)
            o_full[h, lo:hi] = (ot[:, lo:hi] + part).T
            for k in (2, 1, 3, 0):
                x_copy(h, side * 4 + (x + k) % 4).start()

    def chip_sum(h, q):
        x_copy(h, q).wait_recv()
        return o_full[h, owner_rows(q, core)] + cx[h, q]

    def owners_out(h):
        for q in animals_away:
            d_out[h, q] = chip_sum(h, q).astype(BF16)
            d_copy(h, q, mine).start()

    def ridge_column():
        load_r.wait()
        turned = ridge_v[...].T
        for j in range(COLS // BLK):
            ridge_col[j * BLK : (j + 1) * BLK] = turned[:, j : j + 1]

    def finish(h):
        cols = slice(h * HALF, (h + 1) * HALF)
        own = pl.ds(pl.multiple_of(a * OWN, 8), OWN)
        total = chip_sum(h, mine)
        for q in animals_away:
            d_copy(h, q, q).wait_recv()
            total = total + d_in[h, q].astype(F32)
        out[:, cols] = total * (1.0 / math.sqrt(ANIMALS)) + ridge_col[own] * own_v[:, cols].astype(F32)

    def drain_d(h):
        for q in animals_away:
            x_copy(h, q).wait_send()
            d_copy(h, q, mine).wait_send()
        x_copy(h, mine).wait_send()

    def each(count, step):
        def one(i, carry):
            step(i)
            return carry

        lax.fori_loop(0, count, one, 0)

    def step_a(it):
        @pl.when(it + 2 < NC)
        def _():
            load_g(it + 2).start()

        @pl.when(it == NC - 2)
        def _():
            load_p.start()

        product(it)

        @pl.when(it == 0)
        def _():
            pl.semaphore_wait(barrier, PEERS - 1 + len(AWAY))

        reduce1(it)
        pl.when(it >= 2)(lambda: reduce2(it - 2))
        pl.when(it >= 4)(lambda: reduce3(it - 4))

    each(NC, step_a)
    for it in range(NC, NI + 6):
        for i, ring, straight in (
            (it, reduce1, yfirst1),
            (it - 2, reduce2, yfirst2),
            (it - 4, reduce3, lambda i: yfirst3(i, i // NC)),
            (it - 6, lambda i: reduce4(i, i // NC), None),
        ):
            if i < NI and i not in YFIRST:
                ring(i)
            elif i < NI and straight is not None:
                straight(i)
        if it == 2 * NC - 1:
            load_s.wait()
            load_i.wait()
            relatives_out(0)
        if it == 2 * NC:
            ridge_column()
            load_o.wait()
        if it == 2 * NC + 2:
            load_p.wait()
            relatives_in(0)
            relative_sums(0)
    relatives_out(1)
    for c in range(NC - 1):
        relay(c, c % 2 == 0)
    relatives_in(1)
    relative_sums(1)

    def step_m(h, c):
        gather_end(h, c)
        marker_next(h, c)

    gather_end(0, 0)
    marker_first(0)
    step_m(0, 1)
    step_m(0, 2)
    for c in range(NC - 1):
        relay(NC + c, c % 2 == 0)
        if c < NC - 4:
            step_m(0, c + 3)
    gather_end(0, NC - 1)
    marker_last(0)
    gather_end(1, 0)
    marker_first(1)
    owners_out(0)
    each(NC - 2, lambda c: step_m(1, c + 1))
    gather_end(1, NC - 1)
    marker_last(1)
    owners_out(1)
    finish(0)
    finish(1)

    drain_a()
    lax.fori_loop(0, NI, drain_c, 0)
    for h in range(2):
        drain_b(h)
        drain_d(h)


def local(genotypes, direction, ridge, send_list, rel_index, rel_count, rel_prec):
    hbm = pl.BlockSpec(memory_space=pl.ANY)
    smem = pl.BlockSpec(memory_space=pltpu.SMEM)
    vmem = pl.BlockSpec(memory_space=pltpu.VMEM)
    dma = pltpu.SemaphoreType.DMA
    return pl.pallas_call(
        kernel,
        out_shape=jax.ShapeDtypeStruct((OWN, K), F32),
        in_specs=[hbm, hbm, hbm, hbm, hbm, hbm, hbm, smem],
        out_specs=vmem,
        scratch_shapes=[
            pltpu.VMEM((ROWS, COLS), BF16),
            pltpu.VMEM((COLS, K), BF16),
            pltpu.VMEM((OWN, K), BF16),
            pltpu.VMEM((COLS // BLK, BLK), F32),
            pltpu.VMEM((COLS, 1), F32),
            pltpu.VMEM((NB, NREL, BLK, BLK), BF16),
            pltpu.SMEM((SLOTS, PEERS), jnp.int32),
            pltpu.SMEM((NREL, NB), jnp.int32),
            pltpu.VMEM((NC, K, W), F32),
            pltpu.VMEM((NI, KO, W), F32),
            pltpu.VMEM((NI, KO, W), F32),
            pltpu.VMEM((NI, 2 * KO, W), F32),
            pltpu.VMEM((NI, 2 * KO, W), F32),
            pltpu.VMEM((NI, KO, W), F32),
            pltpu.VMEM((len(YFIRST), 4, KO, W), F32),
            pltpu.VMEM((len(YFIRST), 3, KO, W), F32),
            pltpu.VMEM((2, NB, KO, BLK), BF16),
            pltpu.VMEM((NB + PEERS * SLOTS, KO, BLK), BF16),
            pltpu.VMEM((NB + PEERS * SLOTS, KO, BLK), BF16),
            pltpu.VMEM((2, PEERS, SLOTS, KO, BLK), BF16),
            pltpu.VMEM((NC, K, W), BF16),
            pltpu.VMEM((HALF, COLS), F32),
            pltpu.VMEM((2, COLS, HALF), F32),
            pltpu.VMEM((2, 8, OWN, HALF), F32),
            pltpu.VMEM((2, 8, OWN, HALF), BF16),
            pltpu.VMEM((2, 8, OWN, HALF), BF16),
            dma((6,)), dma((NC,)),
            dma((5, NI)), dma((5, NI)),
            dma((7, len(YFIRST))), dma((7, len(YFIRST))),
            dma((2, PEERS)), dma((2, PEERS)),
            dma((7, NI)), dma((7, NI)),
            dma((2, 8)), dma((2, 8)),
            dma((2, 8)), dma((2, 8)),
        ],
        compiler_params=pltpu.CompilerParams(
            collective_id=0, has_side_effects=True, vmem_limit_bytes=63000000
        ),
    )(
        genotypes,
        direction,
        direction.reshape(PEERS, OWN, K),
        ridge.reshape(COLS // BLK, BLK),
        rel_prec,
        send_list[0].T,
        rel_index.T,
        rel_count,
    )


def solution(mesh):
    in_specs = (
        P("animal", "marker"),
        P("marker", None),
        P("marker"),
        P("animal", None, None),
        P("animal", None),
        P("animal"),
        P("animal", None, None, None),
    )
    out_specs = P(("marker", "animal"), None)
    return jax.shard_map(local, mesh=mesh, in_specs=in_specs, out_specs=out_specs, check_vma=False)
```

```python
import math

import jax
import jax.numpy as jnp
from jax import lax
from jax.experimental import pallas as pl
from jax.experimental.pallas import tpu as pltpu
from jax.sharding import PartitionSpec as P

MESH = pl.DeviceIdType.MESH
MARKERS = 25600
ANIMALS = 49152
BLK = 128
K = 256
HALF = 128
NB = 24
NREL = 4
PEERS = 16
SLOTS = 2
ROWS = NB * BLK
COLS = 3200
OWN = 200
KO = 16
CB = 4
W = CB * BLK
NC = NB // CB
SPLIT = 1664
NI = 2 * NC
YFIRST = (6, 11)
AWAY = ((1, 2), (0, 2), (1, 1), (1, 3), (0, 1), (0, 3), (1, 0))
ALONG_Y = 6
RELAYED = ((2, 4), (3, 5), (0, 1))
F32 = jnp.float32
BF16 = jnp.bfloat16


def kernel(
    geno, direc, own_direc, ridge, prec, send_hbm, index_hbm, rel_count, out,
    g_v, d_v, own_v, ridge_v, ridge_col, prec_v, send_list, rel_index, st, r1p, r1m, r2p, r2m, ry, rw, rq, t_loc, table0, table1, stage, rt, ot, o_full, cx,
    d_out, d_in,
    ld_sem, ldg_sem, a_send, a_recv, o_send, o_recv, b_send, b_recv, c_send, c_recv, x_send, x_recv, d_send, d_recv,
):
    a = lax.axis_index("animal")
    m = lax.axis_index("marker")
    z, yh = m // 2, m % 2
    zp, zm, zo = (z + 1) % 4, (z + 3) % 4, (z + 2) % 4
    up, down, across = zp * 2 + yh, zm * 2 + yh, z * 2 + 1 - yh
    core, mine = a % 2, a // 2
    yl, x = mine // 4, mine % 4
    sibling = 2 * mine + 1 - core
    markers_away = [((z + dz) % 4 * 2 + (yh + dy) % 2, (z + 4 - dz) % 4 * 2 + (yh + dy) % 2) for dy, dz in AWAY]
    animals_away = [(yl + dy) % 2 * 4 + (x + dx) % 4 for dy, dx in AWAY]
    tables = (table0, table1)

    def load_g(c):
        rows = pl.ds(pl.multiple_of(c * W, W), W)
        return pltpu.make_async_copy(geno.at[rows], g_v.at[rows], ldg_sem.at[c])

    load_d = pltpu.make_async_copy(direc, d_v, ld_sem.at[0])
    load_p = pltpu.make_async_copy(prec, prec_v, ld_sem.at[1])
    load_s = pltpu.make_async_copy(send_hbm, send_list, ld_sem.at[2])
    load_i = pltpu.make_async_copy(index_hbm, rel_index, ld_sem.at[3])
    load_o = pltpu.make_async_copy(own_direc.at[a], own_v, ld_sem.at[4])
    load_r = pltpu.make_async_copy(ridge, ridge_v, ld_sem.at[5])

    def remote(src, dst, send, recv, **device):
        return pltpu.make_async_remote_copy(
            src_ref=src, dst_ref=dst, send_sem=send, recv_sem=recv, device_id=device, device_id_type=MESH
        )

    load_d.start()
    load_g(0).start()
    barrier = pltpu.get_barrier_semaphore()

    def greet(i, carry):
        pl.semaphore_signal(barrier, inc=1, device_id={"animal": (a + i) % PEERS}, device_id_type=MESH)
        return carry

    lax.fori_loop(1, PEERS, greet, 0)
    for other, _ in markers_away:
        pl.semaphore_signal(barrier, inc=1, device_id={"marker": other}, device_id_type=MESH)
    load_s.start()
    load_i.start()
    load_o.start()
    load_r.start()
    load_d.wait()
    load_g(1).start()

    def krows(i, start, size):
        return pl.ds(pl.multiple_of((i // NC) * HALF + start, KO), size)

    def a1p(i):
        return remote(st.at[i % NC, krows(i, zo * 32, KO)], r1p.at[i], a_send.at[0, i], a_recv.at[0, i], marker=up)

    def a1m(i):
        return remote(st.at[i % NC, krows(i, zo * 32 + KO, KO)], r1m.at[i], a_send.at[1, i], a_recv.at[1, i], marker=down)

    def a2p(i):
        return remote(st.at[i % NC, krows(i, zp * 32, 32)], r2p.at[i], a_send.at[2, i], a_recv.at[2, i], marker=up)

    def a2m(i):
        return remote(st.at[i % NC, krows(i, zm * 32, 32)], r2m.at[i], a_send.at[3, i], a_recv.at[3, i], marker=down)

    def ay(i):
        rows = krows(i, z * 32 + (1 - yh) * KO, KO)
        return remote(st.at[i % NC, rows], ry.at[i], a_send.at[4, i], a_recv.at[4, i], marker=across)

    def product(c):
        load_g(c).wait()
        rows = pl.ds(pl.multiple_of(c * W, W), W)
        st[c] = jnp.dot(g_v[rows, :], d_v[...], preferred_element_type=F32).T

    def reduce1(i):
        a1p(i).start()
        a1m(i).start()

    def reduce2(i):
        a1p(i).wait_recv()
        near = krows(i, zp * 32, KO)
        st[i % NC, near] = st[i % NC, near] + r1p[i]
        a2p(i).start()
        a1m(i).wait_recv()
        near = krows(i, zm * 32 + KO, KO)
        st[i % NC, near] = st[i % NC, near] + r1m[i]
        a2m(i).start()

    def reduce3(i):
        a2p(i).wait_recv()
        a2m(i).wait_recv()
        own = krows(i, z * 32, 32)
        st[i % NC, own] = st[i % NC, own] + (r2p[i] + r2m[i])
        ay(i).start()

    def settle(h, c, done):
        done = (done * (1.0 / math.sqrt(MARKERS))).astype(BF16)
        for b in range(CB):
            t_loc[h, c * CB + b] = done[:, b * BLK : (b + 1) * BLK]
            tables[h][c * CB + b] = done[:, b * BLK : (b + 1) * BLK]

    def reduce4(i, h):
        ay(i).wait_recv()
        settle(h, i % NC, st[i % NC, krows(i, z * 32 + yh * KO, KO)] + ry[i])

    def o_copy(kind, i):
        u = YFIRST.index(i)
        if kind < 4:
            src, dst, to = krows(i, kind * 32 + (1 - yh) * KO, KO), rw.at[u, kind], across
        else:
            to_z = (zo, zp, zm)[kind - 4]
            src, dst, to = krows(i, to_z * 32 + yh * KO, KO), rq.at[u, kind - 4], to_z * 2 + yh
        return remote(st.at[i % NC, src], dst, o_send.at[kind, u], o_recv.at[kind, u], marker=to)

    def yfirst1(i):
        for kind in range(4):
            o_copy(kind, i).start()

    def yfirst2(i):
        u = YFIRST.index(i)
        for kind in range(4):
            o_copy(kind, i).wait_recv()
            own = krows(i, kind * 32 + yh * KO, KO)
            st[i % NC, own] = st[i % NC, own] + rw[u, kind]
        for kind in range(4, 7):
            o_copy(kind, i).start()

    def yfirst3(i, h):
        u = YFIRST.index(i)
        for kind in range(4, 7):
            o_copy(kind, i).wait_recv()
        own = st[i % NC, krows(i, z * 32 + yh * KO, KO)]
        settle(h, i % NC, own + rq[u, 0] + (rq[u, 1] + rq[u, 2]))

    def drain_a():
        for i in range(NI):
            if i in YFIRST:
                for kind in range(7):
                    o_copy(kind, i).wait_send()
            else:
                for copy in (a1p, a1m, a2p, a2m, ay):
                    copy(i).wait_send()

    def b_copy(h, e, p):
        return remote(
            stage.at[h, e], tables[h].at[pl.ds(NB + SLOTS * p, SLOTS)], b_send.at[h, e], b_recv.at[h, p], animal=e
        )

    def relatives_out(h):
        for i in range(1, PEERS):
            e = (a + i) % PEERS
            for s in range(SLOTS):
                stage[h, e, s] = t_loc[h, send_list[s, e]]
            b_copy(h, e, a).start()
        for s in range(SLOTS):
            tables[h][NB + SLOTS * a + s] = t_loc[h, send_list[s, a]]

    def relatives_in(h):
        def one(i, carry):
            p = (a + i) % PEERS
            b_copy(h, p, p).wait_recv()
            return carry

        lax.fori_loop(1, PEERS, one, 0)

    def drain_b(h):
        def one(i, carry):
            b_copy(h, (a + i) % PEERS, a).wait_send()
            return carry

        lax.fori_loop(1, PEERS, one, 0)

    def c_copy(kind, i, owner, to):
        rows = krows(i // NC * NC, owner // 2 * 32 + owner % 2 * KO, KO)
        return remote(rt.at[i % NC, rows], rt.at[i % NC, rows], c_send.at[kind, i], c_recv.at[kind, i], marker=to)

    def c_out(kind, i):
        return c_copy(kind, i, m, markers_away[kind][0])

    def c_in(kind, i):
        return c_copy(kind, i, markers_away[kind][1], m)

    def c_relay(kind, i, zfirst):
        dz = AWAY[kind][1]
        if zfirst:
            return c_copy(kind, i, (z + 4 - dz) % 4 * 2 + yh, across)
        return c_copy(kind, i, across, (z + dz) % 4 * 2 + yh)

    def relay(i, zfirst):
        if not zfirst:
            c_in(ALONG_Y, i).wait_recv()
        for kind, came in RELAYED:
            if zfirst:
                c_in(came, i).wait_recv()
            c_relay(kind, i, zfirst).start()

    def relative_sums(h):
        def one(c, carry):
            i = h * NC + c
            for b in range(CB):
                g = c * CB + b
                count = rel_count[g]
                picked = []
                for j in range(NREL):
                    block = tables[h][rel_index[j, g]]
                    picked.append(jnp.where(j < count, block, jnp.zeros_like(block)))
                total = lax.dot_general(
                    jnp.concatenate(picked, axis=1),
                    jnp.concatenate([prec_v[g, j] for j in range(NREL)], axis=1),
                    (((1,), (1,)), ((), ())),
                    preferred_element_type=F32,
                )
                rt[c, krows(i, m * KO, KO), b * BLK : (b + 1) * BLK] = total.astype(BF16)
            for kind in (1, 4, 5, 6):
                c_out(kind, i).start()

            return carry

        lax.fori_loop(0, NC, one, 0)

    def drain_c(i, carry):
        for kind in range(7):
            c_out(kind, i).wait_send()
        return carry

    def gather_end(h, c):
        i = h * NC + c

        @pl.when(c % 2 == 1)
        def _():
            for kind in (0, 2, 3, ALONG_Y):
                c_in(kind, i).wait_recv()

        @pl.when(c % 2 == 0)
        def _():
            for kind in (0, 1, 2, 3, 4, 5):
                c_in(kind, i).wait_recv()

    def marker_part(h, c):
        rows = pl.ds(pl.multiple_of(c * W, W), W)
        return jnp.dot(rt[c, h * HALF : (h + 1) * HALF], g_v[rows, :], preferred_element_type=F32)

    def marker_first(h):
        ot[...] = marker_part(h, 0)

    def marker_next(h, c):
        ot[...] = ot[...] + marker_part(h, c)

    def owner_rows(q, side):
        return pl.ds(pl.multiple_of((2 * q + side) * OWN, 8), OWN)

    def x_copy(h, q):
        return remote(
            o_full.at[h, owner_rows(q, 1 - core)], cx.at[h, q], x_send.at[h, q], x_recv.at[h, q], animal=sibling
        )

    def d_copy(h, q, sender):
        return remote(d_out.at[h, q], d_in.at[h, sender], d_send.at[h, q], d_recv.at[h, sender], animal=2 * q + core)

    def marker_last(h):
        rows = slice((NC - 1) * W, NC * W)
        for lo, hi, side in ((0, SPLIT, 0), (SPLIT, COLS, 1)):
            part = jnp.dot(rt[NC - 1, h * HALF : (h + 1) * HALF], g_v[rows, lo:hi], preferred_element_type=F32)
            o_full[h, lo:hi] = (ot[:, lo:hi] + part).T
            for k in (2, 1, 3, 0):
                x_copy(h, side * 4 + (x + k) % 4).start()

    def chip_sum(h, q):
        x_copy(h, q).wait_recv()
        return o_full[h, owner_rows(q, core)] + cx[h, q]

    def owners_out(h):
        for q in animals_away:
            d_out[h, q] = chip_sum(h, q).astype(BF16)
            d_copy(h, q, mine).start()

    def ridge_column():
        load_r.wait()
        turned = ridge_v[...].T
        for j in range(COLS // BLK):
            ridge_col[j * BLK : (j + 1) * BLK] = turned[:, j : j + 1]

    def finish(h):
        cols = slice(h * HALF, (h + 1) * HALF)
        own = pl.ds(pl.multiple_of(a * OWN, 8), OWN)
        total = chip_sum(h, mine)
        for q in animals_away:
            d_copy(h, q, q).wait_recv()
            total = total + d_in[h, q].astype(F32)
        out[:, cols] = total * (1.0 / math.sqrt(ANIMALS)) + ridge_col[own] * own_v[:, cols].astype(F32)

    def drain_d(h):
        for q in animals_away:
            x_copy(h, q).wait_send()
            d_copy(h, q, mine).wait_send()
        x_copy(h, mine).wait_send()

    def each(count, step):
        def one(i, carry):
            step(i)
            return carry

        lax.fori_loop(0, count, one, 0)

    def step_a(it):
        @pl.when(it + 2 < NC)
        def _():
            load_g(it + 2).start()

        @pl.when(it == NC - 2)
        def _():
            load_p.start()

        product(it)

        @pl.when(it == 0)
        def _():
            pl.semaphore_wait(barrier, PEERS - 1 + len(AWAY))

        reduce1(it)
        pl.when(it >= 2)(lambda: reduce2(it - 2))
        pl.when(it >= 4)(lambda: reduce3(it - 4))

    each(NC, step_a)
    for it in range(NC, NI + 6):
        for i, ring, straight in (
            (it, reduce1, yfirst1),
            (it - 2, reduce2, yfirst2),
            (it - 4, reduce3, lambda i: yfirst3(i, i // NC)),
            (it - 6, lambda i: reduce4(i, i // NC), None),
        ):
            if i < NI and i not in YFIRST:
                ring(i)
            elif i < NI and straight is not None:
                straight(i)
        if it == 2 * NC - 1:
            load_s.wait()
            load_i.wait()
            relatives_out(0)
        if it == 2 * NC:
            ridge_column()
            load_o.wait()
        if it == 2 * NC + 2:
            load_p.wait()
            relatives_in(0)
            relative_sums(0)
    relatives_out(1)
    for c in range(NC):
        relay(c, c % 2 == 1)
    relatives_in(1)
    relative_sums(1)

    def step_m(h, c):
        gather_end(h, c)
        marker_next(h, c)

    gather_end(0, 0)
    marker_first(0)
    step_m(0, 1)
    step_m(0, 2)
    for c in range(NC):
        relay(NC + c, c % 2 == 1)
        if c < NC - 4:
            step_m(0, c + 3)
    gather_end(0, NC - 1)
    marker_last(0)
    gather_end(1, 0)
    marker_first(1)
    owners_out(0)
    each(NC - 2, lambda c: step_m(1, c + 1))
    gather_end(1, NC - 1)
    marker_last(1)
    owners_out(1)
    finish(0)
    finish(1)

    drain_a()
    lax.fori_loop(0, NI, drain_c, 0)
    for h in range(2):
        drain_b(h)
        drain_d(h)


def local(genotypes, direction, ridge, send_list, rel_index, rel_count, rel_prec):
    hbm = pl.BlockSpec(memory_space=pl.ANY)
    smem = pl.BlockSpec(memory_space=pltpu.SMEM)
    vmem = pl.BlockSpec(memory_space=pltpu.VMEM)
    dma = pltpu.SemaphoreType.DMA
    return pl.pallas_call(
        kernel,
        out_shape=jax.ShapeDtypeStruct((OWN, K), F32),
        in_specs=[hbm, hbm, hbm, hbm, hbm, hbm, hbm, smem],
        out_specs=vmem,
        scratch_shapes=[
            pltpu.VMEM((ROWS, COLS), BF16),
            pltpu.VMEM((COLS, K), BF16),
            pltpu.VMEM((OWN, K), BF16),
            pltpu.VMEM((COLS // BLK, BLK), F32),
            pltpu.VMEM((COLS, 1), F32),
            pltpu.VMEM((NB, NREL, BLK, BLK), BF16),
            pltpu.SMEM((SLOTS, PEERS), jnp.int32),
            pltpu.SMEM((NREL, NB), jnp.int32),
            pltpu.VMEM((NC, K, W), F32),
            pltpu.VMEM((NI, KO, W), F32),
            pltpu.VMEM((NI, KO, W), F32),
            pltpu.VMEM((NI, 2 * KO, W), F32),
            pltpu.VMEM((NI, 2 * KO, W), F32),
            pltpu.VMEM((NI, KO, W), F32),
            pltpu.VMEM((len(YFIRST), 4, KO, W), F32),
            pltpu.VMEM((len(YFIRST), 3, KO, W), F32),
            pltpu.VMEM((2, NB, KO, BLK), BF16),
            pltpu.VMEM((NB + PEERS * SLOTS, KO, BLK), BF16),
            pltpu.VMEM((NB + PEERS * SLOTS, KO, BLK), BF16),
            pltpu.VMEM((2, PEERS, SLOTS, KO, BLK), BF16),
            pltpu.VMEM((NC, K, W), BF16),
            pltpu.VMEM((HALF, COLS), F32),
            pltpu.VMEM((2, COLS, HALF), F32),
            pltpu.VMEM((2, 8, OWN, HALF), F32),
            pltpu.VMEM((2, 8, OWN, HALF), BF16),
            pltpu.VMEM((2, 8, OWN, HALF), BF16),
            dma((6,)), dma((NC,)),
            dma((5, NI)), dma((5, NI)),
            dma((7, len(YFIRST))), dma((7, len(YFIRST))),
            dma((2, PEERS)), dma((2, PEERS)),
            dma((7, NI)), dma((7, NI)),
            dma((2, 8)), dma((2, 8)),
            dma((2, 8)), dma((2, 8)),
        ],
        compiler_params=pltpu.CompilerParams(
            collective_id=0, has_side_effects=True, vmem_limit_bytes=63000000
        ),
    )(
        genotypes,
        direction,
        direction.reshape(PEERS, OWN, K),
        ridge.reshape(COLS // BLK, BLK),
        rel_prec,
        send_list[0].T,
        rel_index.T,
        rel_count,
    )


def solution(mesh):
    in_specs = (
        P("animal", "marker"),
        P("marker", None),
        P("marker"),
        P("animal", None, None),
        P("animal", None),
        P("animal"),
        P("animal", None, None, None),
    )
    out_specs = P(("marker", "animal"), None)
    return jax.shard_map(local, mesh=mesh, in_specs=in_specs, out_specs=out_specs, check_vma=False)
```
